32 devices in a mesh: dp: 8 (over z, x), tensor: 4 (over y, core).
Axes of the slice: x: 2, y: 2, z: 4, core: 2. Of those that a mesh axis runs over, the one named last changes fastest.
Arguments:
- tokens: bfloat16 [16384, 768], P('dp'), may hold values from -6 to 6
- attention_norm_gain: float32 [768], replicated, may hold values from 0.5 to 1.5
- attention_norm_bias: float32 [768], replicated, may hold values from -1 to 1
- feedforward_norm_gain: float32 [768], replicated, may hold values from 0.5 to 1.5
- feedforward_norm_bias: float32 [768], replicated, may hold values from -1 to 1
- w_qkv: bfloat16 [768, 3, 768], P(None, None, 'tensor'), may hold values from -0.3125 to 0.3125
- b_qkv: float32 [3, 768], P(None, 'tensor'), may hold values from -1 to 1
- w_dense: bfloat16 [768, 768], P('tensor'), may hold values from -1.5 to 1.5
- w_fc1: bfloat16 [768, 3072], P(None, 'tensor'), may hold values from -0.21875 to 0.21875
- b_fc1: float32 [3072], P('tensor'), may hold values from -1.5 to 1.5
- w_fc2: bfloat16 [3072, 768], P('tensor'), may hold values from -0.109375 to 0.109375
- out_bias: float32 [768], replicated, may hold values from -1.5 to 1.5
- cotangent: bfloat16 [16384, 768], P('dp'), may hold values from -6 to 6
Outputs:
- block_out: bfloat16 [16384, 768], P('dp')
- grad_tokens: bfloat16 [16384, 768], P('dp')
- attention_gain_gradient: float32 [768], replicated
- grad_shift_one: float32 [768], replicated
- feedforward_gain_gradient: float32 [768], replicated
- grad_shift_two: float32 [768], replicated
- grad_w_qkv: float32 [768, 3, 768], P(None, None, 'tensor')
- grad_b_qkv: float32 [3, 768], P(None, 'tensor')
- grad_w_dense: float32 [768, 768], P('tensor')
- grad_w_fc1: float32 [768, 3072], P(None, 'tensor')
- grad_b_fc1: float32 [3072], P('tensor')
- grad_w_fc2: float32 [3072, 768], P('tensor')
- grad_out_bias: float32 [768], replicated
The draws below stay inside these ranges and needn't reach their ends.
All inputs are finite; a program needn't handle non-finite values.
Results may differ from the reference program's by a relative error of at most 0.006.
The reference program's roundings to bfloat16 on the way count: a program that leaves them out, or rounds other values in their place, can miss the bound.
Values sent between devices are 32-bit elements; how exact they have to be, the bound alone decides.
A program may use at most 128 MiB of HBM per device.

```python
import jax
import jax.numpy as jnp
from jax import lax

D = 768
HEADS = 12
HD = 64
ROT = 16
FF = 3072
LEN = 1024
SEQS = 16
TOKENS = 16384


def level_of(own_key, dims, split, smallest, high):
    level, own = 1.0, jax.random.fold_in(own_key, 6)
    for axis_at, blocks in split:
        steps = jnp.exp(jax.random.uniform(jax.random.fold_in(own, axis_at), (blocks,), jnp.float32, smallest / len(split), high / len(split)))
        level = level * jnp.repeat(steps, dims[axis_at] // blocks).reshape([-1 if axis == axis_at else 1 for axis in range(len(dims))])
    return level


def bell_draw(own_key, dims, deviation, reach, cuts=(), kind=jnp.bfloat16):
    drawn = jax.random.normal(own_key, dims, jnp.float32) * deviation
    if len(cuts) > 0:
        drawn = level_of(own_key, dims, cuts, -0.22, 0.18) * drawn
    return jnp.clip(drawn, min=-reach, max=reach).astype(kind)


def setup_inputs(seed: int = 0) -> dict:
    streams_of = jax.random.split(jax.random.key(seed), 14)
    return {
        "tokens": bell_draw(streams_of[0], (TOKENS, D), 1.0, 6.0, ((0, 8),)),
        "attention_norm_gain": jnp.clip(1.0 + 0.1 * jax.random.normal(streams_of[1], (D,), jnp.float32), 0.5, 1.5),
        "attention_norm_bias": bell_draw(streams_of[2], (D,), 0.2, 1.0, (), jnp.float32),
        "feedforward_norm_gain": jnp.clip(1.0 + 0.1 * jax.random.normal(streams_of[3], (D,), jnp.float32), 0.5, 1.5),
        "feedforward_norm_bias": bell_draw(streams_of[4], (D,), 0.2, 1.0, (), jnp.float32),
        "w_qkv": bell_draw(streams_of[5], (D, 3, D), (D // 2) ** -0.5, 0.3125, ((2, 4),)),
        "b_qkv": bell_draw(streams_of[6], (3, D), 0.2, 1.0, ((1, 4),), jnp.float32),
        "w_dense": bell_draw(streams_of[7], (D, D), (D // 48) ** -0.5, 1.5, ((0, 4),)),
        "w_fc1": bell_draw(streams_of[8], (D, FF), D ** -0.5, 0.21875, ((1, 4),)),
        "b_fc1": bell_draw(streams_of[9], (FF,), 0.3, 1.5, ((0, 4),), jnp.float32),
        "w_fc2": bell_draw(streams_of[10], (FF, D), FF ** -0.5, 0.109375, ((0, 4),)),
        "out_bias": bell_draw(streams_of[11], (D,), 0.3, 1.5, (), jnp.float32),
        "cotangent": bell_draw(streams_of[12], (TOKENS, D), 1.0, 6.0, ((0, 8),)),
    }


@jax.custom_vjp
def low(v):
    return lax.optimization_barrier(v.astype(jnp.bfloat16)).astype(jnp.float32)

@jax.custom_vjp
def low_back(v):
    return v

def low_keep(v):
    return (low(v), None)

def low_pass(kept, grad):
    return (grad,)

def back_keep(v):
    return (v, None)

def back_low(kept, grad):
    return (low(grad),)
low.defvjp(low_keep, low_pass)
low_back.defvjp(back_keep, back_low)

def layer_norm_forward(values_in, norm_gain, norm_bias):
    centered_rows = values_in - lax.optimization_barrier(jnp.mean(values_in, -1, keepdims=True))
    spread = lax.optimization_barrier(jnp.mean(centered_rows * centered_rows, -1, keepdims=True))
    return centered_rows * lax.rsqrt(spread + 1e-05) * norm_gain + norm_bias

def rotation(field, cosine, sine):
    half = ROT // 2
    first = field[..., :half]
    second = field[..., half:ROT]
    return jnp.concatenate([first * cosine - second * sine, second * cosine + first * sine, field[..., ROT:]], -1)

def layer(token_rows, attention_norm_gain, attention_norm_bias, feedforward_norm_gain, feedforward_norm_bias, w_qkv, b_qkv, w_dense, w_fc1, b_fc1, w_fc2, out_bias):
    highest = lax.Precision.HIGHEST
    length = token_rows.shape[0]
    hidden_one = low(layer_norm_forward(token_rows, attention_norm_gain, attention_norm_bias))
    hidden_two = low(layer_norm_forward(token_rows, feedforward_norm_gain, feedforward_norm_bias))
    projected = low_back(jnp.einsum('td,dcf->tcf', hidden_one, w_qkv, precision=highest) + b_qkv[None])
    projected = projected.reshape(length, 3, HEADS, HD)
    position = jnp.arange(length, dtype=jnp.float32)
    freqs = 1.0 / 10000.0 ** (jnp.arange(0, ROT, 2, dtype=jnp.float32) / ROT)
    angle = position[:, None] * freqs[None, :]
    cosine = jnp.cos(angle)[:, None, :]
    sine = jnp.sin(angle)[:, None, :]
    queries = low(rotation(projected[:, 0], cosine, sine))
    key_rows = low(rotation(projected[:, 1], cosine, sine))
    value_rows = low(projected[:, 2])
    raw_scores = low_back(jnp.einsum('qhd,khd->hqk', queries, key_rows, precision=highest))
    places = jnp.arange(length)
    allowed = places[:, None] >= places[None, :]
    scores = jnp.where(allowed[None], raw_scores * HD ** (-0.5), -1e+30)
    probs = low(jax.nn.softmax(scores, axis=-1))
    attended = low_back(low(jnp.einsum('hqk,khd->qhd', probs, value_rows, precision=highest))).reshape(length, D)
    attn_part = jnp.dot(attended, w_dense, precision=highest)
    preact = low_back(jnp.dot(hidden_two, w_fc1, precision=highest) + b_fc1)
    activated = low(jax.nn.gelu(preact, approximate=False))
    mlp_part = jnp.dot(activated, w_fc2, precision=highest)
    return token_rows + (attn_part + mlp_part) + out_bias

def reference(tokens, attention_norm_gain, attention_norm_bias, feedforward_norm_gain, feedforward_norm_bias, w_qkv, b_qkv, w_dense, w_fc1, b_fc1, w_fc2, out_bias, cotangent):
    params = tuple((item.astype(jnp.float32) for item in (attention_norm_gain, attention_norm_bias, feedforward_norm_gain, feedforward_norm_bias, w_qkv, b_qkv, w_dense, w_fc1, b_fc1, w_fc2, out_bias)))
    sentences = tokens.astype(jnp.float32).reshape(SEQS, LEN, D)
    cot_rows = cotangent.astype(jnp.float32).reshape(SEQS, LEN, D)

    def one_sentence(totals, pair):
        sentence, cot_one = pair
        output, pullback = jax.vjp(layer, sentence, *params)
        grads = pullback(cot_one)
        updated = tuple((total + grad for total, grad in zip(totals, grads[1:])))
        return (updated, (output.astype(jnp.bfloat16), grads[0].astype(jnp.bfloat16)))
    start = tuple((jnp.zeros_like(item) for item in params))
    sums, (outputs, grad_rows) = lax.scan(one_sentence, start, (sentences, cot_rows))
    return (outputs.reshape(TOKENS, D), grad_rows.reshape(TOKENS, D), sums[0], sums[1], sums[2], sums[3], sums[4], sums[5], sums[6], sums[7], sums[8], sums[9], sums[10])
```

```python
import math

import jax
import jax.numpy as jnp
import numpy as np
from jax import lax
from jax.experimental import pallas as pl
from jax.experimental.pallas import tpu as pltpu
from jax.sharding import PartitionSpec as P

HD = 64
ROT = 16
LEN = 1024
QB = 256
TB = 256
BF = jnp.bfloat16
F32 = jnp.float32
ROOT_HALF = 0.7071067811865476
ROOT_TAU_INV = 0.3989422804014327
LOG2E = 1.4426950408889634
SCALE = HD ** (-0.5)
VMEM = pltpu.VMEM


def nn(a, b):
    return lax.dot_general(a, b, (((1,), (0,)), ((), ())), preferred_element_type=F32)


def nt(a, b):
    return lax.dot_general(a, b, (((1,), (1,)), ((), ())), preferred_element_type=F32)


def tn(a, b):
    return lax.dot_general(a, b, (((0,), (0,)), ((), ())), preferred_element_type=F32)


def rowsum(v):
    return jnp.sum(v.reshape(v.shape[0] // 8, 8, v.shape[1]), 0)


def standardize(rows):
    x = rows.astype(F32)
    centered = x - jnp.mean(x, -1, keepdims=True)
    inv = lax.rsqrt(jnp.mean(centered * centered, -1, keepdims=True) + 1e-5)
    return centered * inv, inv


def compute_kernel(
    tokens, gain1, bias1, gain2, bias2, wqkvT, bqkv, wdense, wfc1, bfc1, wfc2, cot, cosT, sinT,
    part, cpart, gfc2, gfc1, gdense, gqkvT, vecs, gbqkv,
    hid1, hid2, act, gpre, qT, kT, vT, gAT, qn, kn, vn, gAn, attT, dqT, dk, dv, gT, gn, acc,
):
    tokens_n, D = tokens.shape
    seqs = tokens_n // LEN
    W = wdense.shape[0]
    heads = W // HD
    acc[...] = jnp.zeros_like(acc)

    def tile(i, carry):
        rows = pl.ds(pl.multiple_of(i * TB, TB), TB)
        xhat, _ = standardize(tokens[rows, :])
        hid1[rows, :] = (xhat * gain1[...] + bias1[...]).astype(BF)
        h2 = (xhat * gain2[...] + bias2[...]).astype(BF)
        hid2[rows, :] = h2
        pre = nn(h2, wfc1[...]) + bfc1[...]
        cdf = 0.5 * (1.0 + lax.erf(pre * ROOT_HALF))
        a = (pre * cdf).astype(BF)
        act[rows, :] = a
        slope = cdf + pre * jnp.exp(-0.5 * pre * pre) * ROOT_TAU_INV
        ct = cot[rows, :]
        g = (nt(ct, wfc2[...]) * slope).astype(BF)
        gpre[rows, :] = g
        part[rows, :] = nn(a, wfc2[...])
        g2 = nt(g, wfc1[...])
        cpart[rows, :] = g2 * gain2[...]
        acc[2] += rowsum(g2 * xhat)
        acc[3] += rowsum(g2)
        acc[4] += rowsum(g.astype(F32))
        acc[5] += rowsum(ct.astype(F32))
        return carry

    lax.fori_loop(0, tokens_n // TB, tile, 0)

    def wgrad(lhs, out):
        def body(j, carry):
            cols = pl.ds(pl.multiple_of(j * 256, 256), 256)
            out[cols, :] = tn(lhs[0][:, cols], lhs[1][...])
            return carry

        lax.fori_loop(0, lhs[0].shape[1] // 256, body, 0)

    wgrad((act, cot), gfc2)
    wgrad((hid2, gpre), gfc1)

    for s in range(seqs):
        base = s * LEN

        def proj(j, carry):
            at = pl.multiple_of(j * QB, QB)
            rows = pl.ds(pl.multiple_of(base + at, QB), QB)
            cols = pl.ds(at, QB)
            c, sn = cosT[:, cols], sinT[:, cols]
            pr = nt(wqkvT[...], hid1[rows, :]) + bqkv[...]
            ga = nt(wdense[...], cot[rows, :]).astype(BF)
            gAT[:, cols] = ga
            for h in range(heads):
                for part_at, dT, dn in ((0, qT, qn), (1, kT, kn)):
                    o = part_at * W + h * HD
                    u, w = pr[o : o + 8], pr[o + 8 : o + 16]
                    full = jnp.concatenate(
                        [u * c - w * sn, w * c + u * sn, pr[o + 16 : o + HD]], 0
                    ).astype(BF)
                    dT[h * HD : (h + 1) * HD, cols] = full
                    dn[h, cols, :] = full.T
                o = 2 * W + h * HD
                vv = pr[o : o + HD].astype(BF)
                vT[h * HD : (h + 1) * HD, cols] = vv
                vn[h, cols, :] = vv.T
                gAn[h, cols, :] = ga[h * HD : (h + 1) * HD].T
            return carry

        lax.fori_loop(0, LEN // QB, proj, 0)

        dk[...] = jnp.zeros_like(dk)
        dv[...] = jnp.zeros_like(dv)
        for qb in range(LEN // QB):
            nk = (qb + 1) * QB
            cols = slice(qb * QB, nk)

            def head(h, carry):
                hr = pl.ds(pl.multiple_of(h * HD, HD), HD)
                st = nn(kn[h, :nk, :], qT[hr, cols])
                key = lax.broadcasted_iota(jnp.int32, (QB, QB), 0)
                qry = lax.broadcasted_iota(jnp.int32, (QB, QB), 1)
                diag = jnp.where(key <= qry, st[nk - QB :], -1e30)
                st = jnp.concatenate([st[: nk - QB], diag], 0) if nk > QB else diag
                top = jnp.max(st, 0, keepdims=True)
                e = jnp.exp2((st - top) * (SCALE * LOG2E))
                p = e * (1.0 / jnp.sum(e, 0, keepdims=True))
                low = p.astype(BF)
                attT[hr, cols] = nn(vT[hr, :nk], low).astype(BF)
                gp = nn(vn[h, :nk, :], gAT[hr, cols])
                inner = jnp.sum(p * gp, 0, keepdims=True)
                ds = (p * (gp - inner)).astype(BF)
                dqT[hr, cols] = nn(kT[hr, :nk], ds) * SCALE
                dk[h, :nk, :] += nn(ds, qn[h, cols, :])
                dv[h, :nk, :] += nn(low, gAn[h, cols, :])
                return carry

            lax.fori_loop(0, heads, head, 0)
            rows = pl.ds(base + qb * QB, QB)
            part[rows, :] += tn(attT[:, cols], wdense[...])

        def back(j, carry):
            at = pl.multiple_of(j * QB, QB)
            rows = pl.ds(pl.multiple_of(base + at, QB), QB)
            cols = pl.ds(at, QB)
            c, sn = cosT[:, cols], sinT[:, cols]
            for h in range(heads):
                hs = slice(h * HD, (h + 1) * HD)
                for k, g in (
                    (0, dqT[hs, cols]),
                    (1, dk[h, cols, :].T * SCALE),
                ):
                    u, w = g[0:8], g[8:16]
                    gT[k * W + h * HD : k * W + (h + 1) * HD, cols] = jnp.concatenate(
                        [u * c + w * sn, w * c - u * sn, g[16:]], 0
                    ).astype(BF)
                gT[2 * W + h * HD : 2 * W + (h + 1) * HD, cols] = dv[h, cols, :].T.astype(BF)
            g1 = tn(gT[:, cols], wqkvT[...])
            xhat, _ = standardize(tokens[rows, :])
            cpart[rows, :] += g1 * gain1[...]
            acc[0] += rowsum(g1 * xhat)
            acc[1] += rowsum(g1)
            return carry

        lax.fori_loop(0, LEN // QB, back, 0)
        srows = pl.ds(base, LEN)
        gq = nn(gT[...], hid1[srows, :])
        gd = nn(attT[...], cot[srows, :])
        gb = jnp.sum(gT[...].astype(F32), 1, keepdims=True)
        if s == 0:
            gqkvT[...] = gq
            gdense[...] = gd
            gbqkv[...] = gb
        else:
            gqkvT[...] += gq
            gdense[...] += gd
            gbqkv[...] += gb
    vecs[...] = jnp.sum(acc[...], 1)


def compute(tokens, g1, b1, g2, b2, wqkvT, bqkv, wdense, wfc1, bfc1, wfc2, cot):
    n, D = tokens.shape
    W = wdense.shape[0]
    heads = W // HD
    F = wfc1.shape[1]
    half = ROT // 2
    angle = np.arange(LEN, dtype=np.float64)[None, :] / 10000.0 ** (
        np.arange(0, ROT, 2, dtype=np.float64)[:, None] / ROT
    )
    cosT = jnp.asarray(np.cos(angle), F32)
    sinT = jnp.asarray(np.sin(angle), F32)
    sd = jax.ShapeDtypeStruct
    return pl.pallas_call(
        compute_kernel,
        out_shape=(
            sd((n, D), F32), sd((n, D), F32), sd((F, D), F32), sd((D, F), F32),
            sd((W, D), F32), sd((3 * W, D), F32), sd((8, D), F32), sd((3 * W, 1), F32),
        ),
        scratch_shapes=[
            VMEM((n, D), BF), VMEM((n, D), BF), VMEM((n, F), BF), VMEM((n, F), BF),
            VMEM((W, LEN), BF), VMEM((W, LEN), BF), VMEM((W, LEN), BF), VMEM((W, LEN), BF),
            VMEM((heads, LEN, HD), BF), VMEM((heads, LEN, HD), BF),
            VMEM((heads, LEN, HD), BF), VMEM((heads, LEN, HD), BF),
            VMEM((W, LEN), BF), VMEM((W, LEN), F32),
            VMEM((heads, LEN, HD), F32), VMEM((heads, LEN, HD), F32),
            VMEM((3 * W, LEN), BF), VMEM((8, LEN), F32), VMEM((8, 8, D), F32),
        ],
        compiler_params=pltpu.CompilerParams(vmem_limit_bytes=62 * 2**20),
        name="block",
    )(
        tokens, g1[None], b1[None], g2[None], b2[None], wqkvT, bqkv, wdense, wfc1, bfc1[None],
        wfc2, cot, cosT, sinT,
    )


def on_device(
    tokens, attention_norm_gain, attention_norm_bias, feedforward_norm_gain, feedforward_norm_bias,
    w_qkv, b_qkv, w_dense, w_fc1, b_fc1, w_fc2, out_bias, cotangent,
):
    D = tokens.shape[1]
    W = w_dense.shape[0]
    wqkvT = jnp.transpose(w_qkv, (1, 2, 0)).reshape(3 * W, D)
    part, cpart, gfc2, gfc1, gdense, gqkvT, vecs, gbqkv = compute(
        tokens, attention_norm_gain, attention_norm_bias, feedforward_norm_gain,
        feedforward_norm_bias, wqkvT, b_qkv.reshape(3 * W, 1), w_dense, w_fc1, b_fc1, w_fc2,
        cotangent,
    )
    part, cpart = lax.psum((part, cpart), "tensor")
    block_out = (tokens.astype(F32) + part + out_bias).astype(BF)
    xhat, inv = standardize(tokens)
    grad_tokens = (
        cotangent.astype(F32)
        + inv
        * (
            cpart
            - jnp.mean(cpart, -1, keepdims=True)
            - xhat * jnp.mean(cpart * xhat, -1, keepdims=True)
        )
    ).astype(BF)
    gfc2, gfc1, gdense, gqkvT, gbqkv, vlow = lax.psum(
        (gfc2, gfc1, gdense, gqkvT, gbqkv, vecs[4:6]), "dp"
    )
    vnorm = lax.psum(vecs[:4], ("dp", "tensor"))
    gqkv = jnp.transpose(gqkvT.reshape(3, W, D), (2, 0, 1))
    return (
        block_out, grad_tokens, vnorm[0], vnorm[1], vnorm[2], vnorm[3], gqkv,
        gbqkv.reshape(3, W), gdense, gfc1, vlow[0], gfc2, vlow[1],
    )


def solution(mesh):
    placed = (
        P("dp", None), P(), P(), P(), P(), P(None, None, "tensor"), P(None, "tensor"),
        P("tensor", None), P(None, "tensor"), P("tensor"), P("tensor", None), P(), P("dp", None),
    )
    return jax.shard_map(
        on_device, mesh=mesh, in_specs=placed,
        out_specs=(
            P("dp", None), P("dp", None), P(), P(), P(), P(), P(None, None, "tensor"),
            P(None, "tensor"), P("tensor", None), P(None, "tensor"), P("tensor"),
            P("tensor", None), P(),
        ),
        check_vma=False,
    )
```

```python
import math

import jax
import jax.numpy as jnp
import numpy as np
from jax import lax
from jax.experimental import pallas as pl
from jax.experimental.pallas import tpu as pltpu
from jax.sharding import PartitionSpec as P

HD = 64
ROT = 16
LEN = 1024
QB = 256
TB = 256
CH = 256
RC = 48
SLOTS = 8
RING = 6
MESH = pl.DeviceIdType.MESH
BF = jnp.bfloat16
F32 = jnp.float32
ROOT_HALF = 0.7071067811865476
ROOT_TAU_INV = 0.3989422804014327
LOG2E = 1.4426950408889634
SCALE = HD ** (-0.5)
VMEM = pltpu.VMEM


def nn(a, b):
    return lax.dot_general(a, b, (((1,), (0,)), ((), ())), preferred_element_type=F32)


def nt(a, b):
    return lax.dot_general(a, b, (((1,), (1,)), ((), ())), preferred_element_type=F32)


def tn(a, b):
    return lax.dot_general(a, b, (((0,), (0,)), ((), ())), preferred_element_type=F32)


def rowsum(v):
    return jnp.sum(v.reshape(v.shape[0] // 8, 8, v.shape[1]), 0)


def standardize(rows):
    x = rows.astype(F32)
    centered = x - jnp.mean(x, -1, keepdims=True)
    inv = lax.rsqrt(jnp.mean(centered * centered, -1, keepdims=True) + 1e-5)
    return centered * inv, inv


def when(cond, f):
    pl.when(cond)(f)


class Ranks:
    def __init__(self, grid):
        t = lax.axis_index("tensor")
        d = lax.axis_index("dp")
        self.core = t % 2
        self.sib = {"tensor": t + 1 - 2 * (t % 2)}
        self.ypeer = {"tensor": (t + 2) % 4}
        self.x = d % 2
        z = d // 2
        self.xpeer = {"dp": d + 1 - 2 * (d % 2)}
        self.zpeer = {"dp": d + 2 - 4 * (z % 2)}
        self.mpeer = {"dp": (3 - z) * 2 + d % 2}
        self.center = ((z + 1) // 2) % 2
        self.hm = (z // 2) % 2
        self.grid = grid

    def barrier(self):
        peers = [self.sib, self.ypeer]
        if self.grid:
            peers += [self.xpeer, self.zpeer, self.mpeer]
        sem = pltpu.get_barrier_semaphore()
        for peer in peers:
            pl.semaphore_signal(sem, inc=1, device_id=peer, device_id_type=MESH)
        pl.semaphore_wait(sem, len(peers))


def at(start, size):
    return pl.ds(pl.multiple_of(start, 8), size)


def copy(src, dst, send, recv, peer):
    return pltpu.make_async_remote_copy(
        src_ref=src, dst_ref=dst, send_sem=send, recv_sem=recv, device_id=peer,
        device_id_type=MESH,
    )


def tell(sem, peer):
    pl.semaphore_signal(sem, inc=1, device_id=peer, device_id_type=MESH)


def add_into(dst, rows, src, srows):
    dst[rows, :] = dst[rows, :] + src[srows, :]


class TensorSum:
    HALF = CH // 2

    def __init__(self, rank, pc, rc1, rc2, send, recv, free):
        self.r, self.pc, self.rc1, self.rc2 = rank, pc, rc1, rc2
        self.s, self.v, self.free = send, recv, free
        self.n = pc.shape[0] // CH

    def mine(self, j):
        return at(j * CH + self.r.core * self.HALF, self.HALF)

    def other(self, j):
        return at(j * CH + (1 - self.r.core) * self.HALF, self.HALF)

    def slot(self, j):
        return at((j % SLOTS) * self.HALF, self.HALF)

    def land(self, j):
        return at(j * self.HALF, self.HALF)

    def c1(self, j):
        return copy(self.pc.at[self.other(j), :], self.rc1.at[self.slot(j), :],
                    self.s.at[0, j], self.v.at[0, j], self.r.sib)

    def c2(self, j):
        return copy(self.pc.at[self.mine(j), :], self.rc2.at[self.land(j), :],
                    self.s.at[1, j], self.v.at[1, j], self.r.ypeer)

    def c3(self, j):
        return copy(self.pc.at[self.mine(j), :], self.pc.at[self.mine(j), :],
                    self.s.at[2, j], self.v.at[2, j], self.r.sib)

    def y1(self, j):
        self.c1(j).start()

    def y2(self, j):
        self.c1(j).wait_recv()
        add_into(self.pc, self.mine(j), self.rc1, self.slot(j))
        self.c2(j).start()
        self.c1(j).wait_send()
        tell(self.free, self.r.sib)

    def y3(self, j, finish):
        self.c2(j).wait()
        add_into(self.pc, self.mine(j), self.rc2, self.land(j))
        pl.semaphore_wait(self.free, 1)
        self.c3(j).start()
        finish(j, self.r.core)

    def y4(self, j, finish, flush):
        self.c3(j).wait()
        finish(j, 1 - self.r.core)
        flush(j)


class GradSum:
    HALF = RC // 2

    def __init__(self, rank, g, ax, az, am, bz, bm, bx, a_s, a_r, b_s, b_r, free, na, nb, flush):
        self.r, self.g = rank, g
        self.ax, self.az, self.am, self.bz, self.bm, self.bx = ax, az, am, bz, bm, bx
        self.a_s, self.a_r, self.b_s, self.b_r = a_s, a_r, b_s, b_r
        self.na, self.nb, self.flush, self.free = na, nb, flush, free

    def amine(self, k):
        return at(2 * k * RC + self.r.x * self.HALF, self.HALF)

    def aother(self, k):
        return at(2 * k * RC + (1 - self.r.x) * self.HALF, self.HALF)

    def buf(self, k):
        return at((k % RING) * self.HALF, self.HALF)

    def zbuf(self, k):
        return at((k % RING) * RC, RC)

    def ac(self, kind, k):
        g, m, b = self.g, self.amine(k), self.buf(k)
        src, dst, peer = (
            (g.at[self.aother(k), :], self.ax.at[b, :], self.r.xpeer),
            (g.at[m, :], self.az.at[b, :], self.r.zpeer),
            (g.at[m, :], self.am.at[b, :], self.r.mpeer),
            (g.at[m, :], g.at[m, :], self.r.zpeer),
            (g.at[m, :], g.at[m, :], self.r.xpeer),
        )[kind]
        return copy(src, dst, self.a_s.at[kind, k], self.a_r.at[kind, k], peer)

    def a1(self, k):
        self.ac(0, k).start()

    def a2(self, k):
        self.ac(0, k).wait_recv()
        add_into(self.g, self.amine(k), self.ax, self.buf(k))
        when(self.r.center == 0, lambda: self.ac(1, k).start())
        self.ac(0, k).wait_send()
        tell(self.free.at[0], self.r.xpeer)

    def a3(self, k):
        @pl.when(self.r.center == 1)
        def _():
            self.ac(1, k).wait_recv()
            add_into(self.g, self.amine(k), self.az, self.buf(k))
            self.ac(2, k).start()

        @pl.when(self.r.center == 0)
        def _():
            self.ac(1, k).wait_send()
            tell(self.free.at[1], self.r.zpeer)

    def a4(self, k):
        @pl.when(self.r.center == 1)
        def _():
            self.ac(2, k).wait()
            add_into(self.g, self.amine(k), self.am, self.buf(k))
            pl.semaphore_wait(self.free.at[1], 1)
            self.ac(3, k).start()
            pl.semaphore_wait(self.free.at[0], 1)
            self.ac(4, k).start()

    def a5(self, k):
        @pl.when(self.r.center == 0)
        def _():
            self.ac(3, k).wait_recv()
            pl.semaphore_wait(self.free.at[0], 1)
            self.ac(4, k).start()

    def a6(self, k):
        self.ac(4, k).wait()
        when(self.r.center == 1, lambda: self.ac(3, k).wait_send())
        self.flush(2 * k * RC, RC, 2 * k).start()

    def bfull(self, k):
        return at((2 * k + 1) * RC, RC)

    def bmine(self, k):
        return at((2 * k + 1) * RC + self.r.hm * self.HALF, self.HALF)

    def bother(self, k):
        return at((2 * k + 1) * RC + (1 - self.r.hm) * self.HALF, self.HALF)

    def bc(self, kind, k):
        g, f, m, o, b = self.g, self.bfull(k), self.bmine(k), self.bother(k), self.buf(k)
        src, dst, peer = (
            (g.at[f, :], self.bz.at[self.zbuf(k), :], self.r.zpeer),
            (g.at[o, :], self.bm.at[b, :], self.r.mpeer),
            (g.at[m, :], self.bx.at[b, :], self.r.xpeer),
            (g.at[m, :], g.at[m, :], self.r.mpeer),
            (g.at[m, :], g.at[m, :], self.r.zpeer),
            (g.at[o, :], g.at[o, :], self.r.zpeer),
        )[kind]
        return copy(src, dst, self.b_s.at[kind, k], self.b_r.at[kind, k], peer)

    def b1(self, k):
        when(self.r.center == 0, lambda: self.bc(0, k).start())

    def b2(self, k):
        @pl.when(self.r.center == 1)
        def _():
            self.bc(0, k).wait_recv()
            add_into(self.g, self.bfull(k), self.bz, self.zbuf(k))
            self.bc(1, k).start()

        @pl.when(self.r.center == 0)
        def _():
            self.bc(0, k).wait_send()
            tell(self.free.at[2], self.r.zpeer)

    def b3(self, k):
        @pl.when(self.r.center == 1)
        def _():
            self.bc(1, k).wait_recv()
            add_into(self.g, self.bmine(k), self.bm, self.buf(k))
            self.bc(2, k).start()
            self.bc(1, k).wait_send()
            tell(self.free.at[3], self.r.mpeer)

    def b4(self, k):
        @pl.when(self.r.center == 1)
        def _():
            self.bc(2, k).wait()
            add_into(self.g, self.bmine(k), self.bx, self.buf(k))
            pl.semaphore_wait(self.free.at[3], 1)
            self.bc(3, k).start()
            pl.semaphore_wait(self.free.at[2], 1)
            self.bc(4, k).start()

    def b5(self, k):
        @pl.when(self.r.center == 1)
        def _():
            self.bc(3, k).wait_recv()
            self.bc(5, k).start()

    def b6(self, k):
        @pl.when(self.r.center == 1)
        def _():
            self.bc(3, k).wait_send()
            self.bc(4, k).wait_send()
            self.bc(5, k).wait_send()

        @pl.when(self.r.center == 0)
        def _():
            self.bc(4, k).wait_recv()
            self.bc(5, k).wait_recv()

        self.flush((2 * k + 1) * RC, RC, 2 * k + 1).start()

    def tick(self, t):
        for n, stages in ((self.nb, (self.b1, self.b2, self.b3, self.b4, self.b5, self.b6)),
                          (self.na, (self.a1, self.a2, self.a3, self.a4, self.a5, self.a6))):
            for back in range(5, -1, -1):
                k = t - back
                when(jnp.logical_and(k >= 0, k < n), lambda f=stages[back], k=k: f(k))


def block_kernel(
    grid, tokens, gain1, bias1, gain2, bias2, wqkvT, bqkv, wdense, wfc1, bfc1, wfc2, obias, cot,
    cosT, sinT,
    blk_out, gtok_out, grad_out,
    hid2, act, gpre, qT, kT, vT, gAT, qn, kn, vn, gAn, attT, dqT, dk, dv, gT, acc,
    pc, g, rc1, rc2, vs, vr1, vr2, ax, az, am, bz, bm, bx,
    y_s, y_r, v_s, v_r, a_s, a_r, b_s, b_r, o_s, g_s, y_f, d_f,
):
    n, D = tokens.shape
    seqs = n // LEN
    W = wdense.shape[0]
    F = wfc1.shape[1]
    heads = W // HD
    nblk = n // CH
    na, nb = a_s.shape[1], b_s.shape[1]
    r_fc2, r_fc1, r_qkv, r_dense, r_vec = 0, F, F + D, F + D + 3 * W, F + D + 4 * W
    rank = Ranks(grid)
    rank.barrier()
    ts = TensorSum(rank, pc, rc1, rc2, y_s, y_r, y_f)
    blk, gtok = hid2, act

    def flush_grad(row, size, i):
        return pltpu.make_async_copy(g.at[at(row, size), :], grad_out.at[at(row, size), :], g_s.at[i])

    gs = GradSum(rank, g, ax, az, am, bz, bm, bx, a_s, a_r, b_s, b_r, d_f, na, nb, flush_grad)

    def dp_ticks(first, count):
        if grid:
            lax.fori_loop(first, first + count, lambda t, c: (gs.tick(t), c)[1], 0)

    acc[...] = jnp.zeros_like(acc)
    g[at(r_qkv, g.shape[0] - r_qkv), :] = jnp.zeros((g.shape[0] - r_qkv, D), F32)

    def tile(i, carry):
        rows = at(i * TB, TB)
        xhat, _ = standardize(tokens[rows, :])
        h2 = (xhat * gain2[...] + bias2[...]).astype(BF)
        hid2[rows, :] = h2
        pre = nn(h2, wfc1[...]) + bfc1[...]
        cdf = 0.5 * (1.0 + lax.erf(pre * ROOT_HALF))
        a = (pre * cdf).astype(BF)
        act[rows, :] = a
        slope = cdf + pre * jnp.exp(-0.5 * pre * pre) * ROOT_TAU_INV
        ct = cot[rows, :]
        gp = (nt(ct, wfc2[...]) * slope).astype(BF)
        gpre[rows, :] = gp
        pc[rows, :] = nn(a, wfc2[...])
        g2 = nt(gp, wfc1[...])
        pc[at(n + i * TB, TB), :] = g2 * gain2[...]
        acc[2] += rowsum(g2 * xhat)
        acc[3] += rowsum(g2)
        acc[4] += rowsum(gp.astype(F32))
        acc[5] += rowsum(ct.astype(F32))
        return carry

    lax.fori_loop(0, n // TB, tile, 0)

    def wgrad(lhs, rhs, row):
        def body(j, carry):
            g[at(row + j * 256, 256), :] = tn(lhs[:, pl.ds(pl.multiple_of(j * 256, 256), 256)], rhs[...])
            return carry

        lax.fori_loop(0, lhs.shape[1] // 256, body, 0)

    wgrad(act, cot, r_fc2)
    wgrad(hid2, gpre, r_fc1)

    def sentence(s, carry):
        base = s * LEN

        def proj(j, carry):
            cols = pl.ds(pl.multiple_of(j * QB, QB), QB)
            rows = at(base + j * QB, QB)
            c, sn = cosT[:, cols], sinT[:, cols]
            xhat, _ = standardize(tokens[rows, :])
            h1 = (xhat * gain1[...] + bias1[...]).astype(BF)
            gpre[rows, :] = h1
            pr = nt(wqkvT[...], h1) + bqkv[...]
            ga = nt(wdense[...], cot[rows, :]).astype(BF)
            gAT[:, cols] = ga
            for h in range(heads):
                for part, dT, dn in ((0, qT, qn), (1, kT, kn)):
                    o = part * W + h * HD
                    u, w = pr[o : o + 8], pr[o + 8 : o + 16]
                    full = jnp.concatenate(
                        [u * c - w * sn, w * c + u * sn, pr[o + 16 : o + HD]], 0
                    ).astype(BF)
                    dT[h * HD : (h + 1) * HD, cols] = full
                    dn[h, cols, :] = full.T
                o = 2 * W + h * HD
                vv = pr[o : o + HD].astype(BF)
                vT[h * HD : (h + 1) * HD, cols] = vv
                vn[h, cols, :] = vv.T
                gAn[h, cols, :] = ga[h * HD : (h + 1) * HD].T
            return carry

        lax.fori_loop(0, LEN // QB, proj, 0)

        dk[...] = jnp.zeros_like(dk)
        dv[...] = jnp.zeros_like(dv)
        for qb in range(LEN // QB):
            nk = (qb + 1) * QB
            cols = slice(qb * QB, nk)

            def head(h, carry):
                hr = pl.ds(pl.multiple_of(h * HD, HD), HD)
                st = nn(kn[h, :nk, :], qT[hr, cols])
                key = lax.broadcasted_iota(jnp.int32, (QB, QB), 0)
                qry = lax.broadcasted_iota(jnp.int32, (QB, QB), 1)
                diag = jnp.where(key <= qry, st[nk - QB :], -1e30)
                st = jnp.concatenate([st[: nk - QB], diag], 0) if nk > QB else diag
                top = jnp.max(st, 0, keepdims=True)
                e = jnp.exp2((st - top) * (SCALE * LOG2E))
                p = e * (1.0 / jnp.sum(e, 0, keepdims=True))
                low = p.astype(BF)
                attT[hr, cols] = nn(vT[hr, :nk], low).astype(BF)
                gp = nn(vn[h, :nk, :], gAT[hr, cols])
                inner = jnp.sum(p * gp, 0, keepdims=True)
                ds = (p * (gp - inner)).astype(BF)
                dqT[hr, cols] = nn(kT[hr, :nk], ds) * SCALE
                dk[h, :nk, :] += nn(ds, qn[h, cols, :])
                dv[h, :nk, :] += nn(low, gAn[h, cols, :])
                return carry

            lax.fori_loop(0, heads, head, 0)
            pc[at(base + qb * QB, QB), :] += tn(attT[:, cols], wdense[...])
            j = s * (LEN // QB) + qb
            ts.y1(j)
            when(j > 0, lambda j=j: ts.y2(j - 1))

        def back(j, carry):
            cols = pl.ds(pl.multiple_of(j * QB, QB), QB)
            rows = at(base + j * QB, QB)
            c, sn = cosT[:, cols], sinT[:, cols]
            for h in range(heads):
                hs = slice(h * HD, (h + 1) * HD)
                for k, gr in ((0, dqT[hs, cols]), (1, dk[h, cols, :].T * SCALE)):
                    u, w = gr[0:8], gr[8:16]
                    gT[k * W + h * HD : k * W + (h + 1) * HD, cols] = jnp.concatenate(
                        [u * c + w * sn, w * c - u * sn, gr[16:]], 0
                    ).astype(BF)
                gT[2 * W + h * HD : 2 * W + (h + 1) * HD, cols] = dv[h, cols, :].T.astype(BF)
            g1 = tn(gT[:, cols], wqkvT[...])
            xhat, _ = standardize(tokens[rows, :])
            pc[at(n + base + j * QB, QB), :] += g1 * gain1[...]
            acc[0] += rowsum(g1 * xhat)
            acc[1] += rowsum(g1)
            return carry

        lax.fori_loop(0, LEN // QB, back, 0)
        srows = at(base, LEN)
        g[at(r_qkv, 3 * W), :] += nn(gT[...], gpre[srows, :])
        g[at(r_dense, W), :] += nn(attT[...], cot[srows, :])
        ones = jnp.ones((8, LEN), BF)
        g[r_vec + 6 : r_vec + 7, 0 : 3 * W] += nt(ones, gT[...])[0:1]
        return carry

    lax.fori_loop(0, seqs, sentence, 0)
    ts.y2(nblk - 1)

    vs[...] = jnp.sum(acc[...], 1)
    v1 = copy(vs, vr1, v_s.at[0], v_r.at[0], rank.sib)
    v1.start()
    g[r_vec + 4 : r_vec + 6, :] = vs[4:6, :]
    v1.wait()
    vs[...] = vs[...] + vr1[...]
    v2 = copy(vs, vr2, v_s.at[1], v_r.at[1], rank.ypeer)
    v2.start()
    v2.wait()
    g[r_vec : r_vec + 4, :] = vs[0:4, :] + vr2[0:4, :]

    def finish_block(j, half):
        rows = at(j * CH + half * (CH // 2), CH // 2)
        blk[rows, :] = (tokens[rows, :].astype(F32) + pc[rows, :] + obias[...]).astype(BF)

    def finish_tokens(j, half):
        rows = at((j - nblk) * CH + half * (CH // 2), CH // 2)
        c = pc[at(j * CH + half * (CH // 2), CH // 2), :]
        xhat, inv = standardize(tokens[rows, :])
        inside = c - jnp.mean(c, -1, keepdims=True) - xhat * jnp.mean(c * xhat, -1, keepdims=True)
        gtok[rows, :] = (cot[rows, :].astype(F32) + inv * inside).astype(BF)

    def out_copy(j, src, dst, first):
        rows = at((j - first) * CH, CH)
        return pltpu.make_async_copy(src.at[rows, :], dst.at[rows, :], o_s.at[j])

    def flush_block(j):
        out_copy(j, blk, blk_out, 0).start()

    def flush_tokens(j):
        out_copy(j, gtok, gtok_out, nblk).start()

    LEAD = 6

    def drain(u, carry):
        when(jnp.logical_and(u >= 1, u <= nblk), lambda: ts.y4(u - 1, finish_block, flush_block))
        when(u > nblk, lambda: ts.y4(u - 1, finish_tokens, flush_tokens))
        when(u < nblk, lambda: ts.y3(u, finish_block))
        when(jnp.logical_and(u >= nblk, u < 2 * nblk), lambda: ts.y3(u, finish_tokens))
        when(jnp.logical_and(u + LEAD - 1 >= nblk, u + LEAD - 1 < 2 * nblk), lambda: ts.y2(u + LEAD - 1))
        when(jnp.logical_and(u + LEAD >= nblk, u + LEAD < 2 * nblk), lambda: ts.y1(u + LEAD))
        dp_ticks(2 * u, 2)
        return carry

    steps = max(2 * nblk + 1, (max(na, nb) + 6) // 2 if grid else 0)
    lax.fori_loop(0, steps, drain, 0)

    def landed(j, carry):
        out_copy(j, blk, blk_out, 0).wait()
        out_copy(j + nblk, gtok, gtok_out, nblk).wait()
        return carry

    lax.fori_loop(0, nblk, landed, 0)
    if grid:
        lax.fori_loop(0, na + nb, lambda i, c: (flush_grad(i * RC, RC, i).wait(), c)[1], 0)
    else:
        whole = flush_grad(0, g.shape[0], 0)
        whole.start()
        whole.wait()


def block(grid, tokens, vectors, wqkvT, bqkv, wdense, wfc1, wfc2, cot):
    n, D = tokens.shape
    W = wdense.shape[0]
    heads = W // HD
    F = wfc1.shape[1]
    angle = np.arange(LEN, dtype=np.float64)[None, :] / 10000.0 ** (
        np.arange(0, ROT, 2, dtype=np.float64)[:, None] / ROT
    )
    cosT = jnp.asarray(np.cos(angle), F32)
    sinT = jnp.asarray(np.sin(angle), F32)
    g1, b1, g2, b2, bfc1, ob = (v[None] for v in vectors)
    pairs = (F + D + 4 * W) // (2 * RC)
    na, nb = pairs + 1, pairs
    rows = (na + nb) * RC
    half, DMA = RC // 2, pltpu.SemaphoreType.DMA
    sd = jax.ShapeDtypeStruct
    inputs = (tokens, g1, b1, g2, b2, wqkvT, bqkv, wdense, wfc1, bfc1, wfc2, ob, cot, cosT, sinT)
    nch = 2 * n // CH
    return pl.pallas_call(
        lambda *refs: block_kernel(grid, *refs),
        out_shape=(sd((n, D), BF), sd((n, D), BF), sd((rows, D), F32)),
        in_specs=[pl.BlockSpec(memory_space=VMEM)] * len(inputs),
        out_specs=[pl.BlockSpec(memory_space=pl.ANY)] * 3,
        scratch_shapes=[
            VMEM((n, D), BF), VMEM((n, F), BF), VMEM((n, F), BF),
            VMEM((W, LEN), BF), VMEM((W, LEN), BF), VMEM((W, LEN), BF), VMEM((W, LEN), BF),
            VMEM((heads, LEN, HD), BF), VMEM((heads, LEN, HD), BF),
            VMEM((heads, LEN, HD), BF), VMEM((heads, LEN, HD), BF),
            VMEM((W, LEN), BF), VMEM((W, LEN), F32),
            VMEM((heads, LEN, HD), F32), VMEM((heads, LEN, HD), F32),
            VMEM((3 * W, LEN), BF), VMEM((8, 8, D), F32),
            VMEM((2 * n, D), F32), VMEM((rows, D), F32),
            VMEM((SLOTS * CH // 2, D), F32), VMEM((nch * CH // 2, D), F32),
            VMEM((8, D), F32), VMEM((8, D), F32), VMEM((8, D), F32),
            VMEM((RING * half, D), F32), VMEM((RING * half, D), F32), VMEM((RING * half, D), F32),
            VMEM((RING * RC, D), F32), VMEM((RING * half, D), F32), VMEM((RING * half, D), F32),
            DMA((3, nch)), DMA((3, nch)), DMA((2,)), DMA((2,)),
            DMA((5, na)), DMA((5, na)), DMA((6, nb)), DMA((6, nb)), DMA((nch,)), DMA((na + nb,)),
            pltpu.SemaphoreType.REGULAR, pltpu.SemaphoreType.REGULAR((4,)),
        ],
        compiler_params=pltpu.CompilerParams(
            vmem_limit_bytes=63 * 2**20, collective_id=0, has_side_effects=True
        ),
        name="block",
    )(*inputs)


def on_device(
    grid, tokens, attention_norm_gain, attention_norm_bias, feedforward_norm_gain,
    feedforward_norm_bias, w_qkv, b_qkv, w_dense, w_fc1, b_fc1, w_fc2, out_bias, cotangent,
):
    D = tokens.shape[1]
    W, F = w_dense.shape[0], w_fc1.shape[1]
    wqkvT = jnp.transpose(w_qkv, (1, 2, 0)).reshape(3 * W, D)
    vectors = (
        attention_norm_gain, attention_norm_bias, feedforward_norm_gain, feedforward_norm_bias,
        b_fc1, out_bias,
    )
    block_out, grad_tokens, grads = block(
        grid, tokens, vectors, wqkvT, b_qkv.reshape(3 * W, 1), w_dense, w_fc1, w_fc2, cotangent
    )
    if not grid:
        grads = lax.psum(grads, "dp")
    gfc2, gfc1 = grads[:F], grads[F : F + D]
    gqkv = jnp.transpose(grads[F + D : F + D + 3 * W].reshape(3, W, D), (2, 0, 1))
    gdense = grads[F + D + 3 * W : F + D + 4 * W]
    v = grads[F + D + 4 * W :]
    return (
        block_out, grad_tokens, v[0], v[1], v[2], v[3], gqkv, v[6, : 3 * W].reshape(3, W), gdense,
        gfc1, v[4], gfc2, v[5],
    )


def solution(mesh):
    placed = (
        P("dp", None), P(), P(), P(), P(), P(None, None, "tensor"), P(None, "tensor"),
        P("tensor", None), P(None, "tensor"), P("tensor"), P("tensor", None), P(), P("dp", None),
    )
    grid = mesh.shape["dp"] == 8
    return jax.shard_map(
        lambda *args: on_device(grid, *args), mesh=mesh, in_specs=placed,
        out_specs=(
            P("dp", None), P("dp", None), P(), P(), P(), P(), P(None, None, "tensor"),
            P(None, "tensor"), P("tensor", None), P(None, "tensor"), P("tensor"),
            P("tensor", None), P(),
        ),
        check_vma=False,
    )
```

```python
import math

import jax
import jax.numpy as jnp
import numpy as np
from jax import lax
from jax.experimental import pallas as pl
from jax.experimental.pallas import tpu as pltpu
from jax.sharding import PartitionSpec as P

HD = 64
ROT = 16
LEN = 1024
QB = 256
TB = 256
CH = 256
RC = 48
SLOTS = 8
RING = 6
SCOPED = 50 * 2**20
TICKS = ((None, 0), (None, 1), (2, 3), (4, 5))
PER = 7
MESH = pl.DeviceIdType.MESH
BF = jnp.bfloat16
F32 = jnp.float32
ROOT_HALF = 0.7071067811865476
ROOT_TAU_INV = 0.3989422804014327
LOG2E = 1.4426950408889634
SCALE = HD ** (-0.5)
VMEM = pltpu.VMEM


def nn(a, b):
    return lax.dot_general(a, b, (((1,), (0,)), ((), ())), preferred_element_type=F32)


def nt(a, b):
    return lax.dot_general(a, b, (((1,), (1,)), ((), ())), preferred_element_type=F32)


def tn(a, b):
    return lax.dot_general(a, b, (((0,), (0,)), ((), ())), preferred_element_type=F32)


def rowsum(v):
    return jnp.sum(v.reshape(v.shape[0] // 8, 8, v.shape[1]), 0)


def standardize(rows):
    x = rows.astype(F32)
    centered = x - jnp.mean(x, -1, keepdims=True)
    inv = lax.rsqrt(jnp.mean(centered * centered, -1, keepdims=True) + 1e-5)
    return centered * inv, inv


def when(cond, f):
    pl.when(cond)(f)


class Ranks:
    def __init__(self, grid):
        t = lax.axis_index("tensor")
        d = lax.axis_index("dp")
        self.core = t % 2
        self.sib = {"tensor": t + 1 - 2 * (t % 2)}
        self.ypeer = {"tensor": (t + 2) % 4}
        self.x = d % 2
        z = d // 2
        self.xpeer = {"dp": d + 1 - 2 * (d % 2)}
        self.zpeer = {"dp": d + 2 - 4 * (z % 2)}
        self.mpeer = {"dp": (3 - z) * 2 + d % 2}
        self.center = ((z + 1) // 2) % 2
        self.hm = (z // 2) % 2
        self.grid = grid

    def barrier(self):
        peers = [self.sib, self.ypeer]
        if self.grid:
            peers += [self.xpeer, self.zpeer, self.mpeer]
        sem = pltpu.get_barrier_semaphore()
        for peer in peers:
            pl.semaphore_signal(sem, inc=1, device_id=peer, device_id_type=MESH)
        pl.semaphore_wait(sem, len(peers))


def at(start, size):
    return pl.ds(pl.multiple_of(start, 8), size)


def copy(src, dst, send, recv, peer):
    return pltpu.make_async_remote_copy(
        src_ref=src, dst_ref=dst, send_sem=send, recv_sem=recv, device_id=peer,
        device_id_type=MESH,
    )


def tell(sem, peer):
    pl.semaphore_signal(sem, inc=1, device_id=peer, device_id_type=MESH)


def add_into(dst, rows, src, srows):
    dst[rows, :] = dst[rows, :] + src[srows, :]


class TensorSum:
    HALF = CH // 2

    def __init__(self, rank, pc, rc1, rc2, send, recv, free):
        self.r, self.pc, self.rc1, self.rc2 = rank, pc, rc1, rc2
        self.s, self.v, self.free = send, recv, free
        self.n = pc.shape[0] // CH

    def mine(self, j):
        return at(j * CH + self.r.core * self.HALF, self.HALF)

    def other(self, j):
        return at(j * CH + (1 - self.r.core) * self.HALF, self.HALF)

    def slot(self, j):
        return at((j % SLOTS) * self.HALF, self.HALF)

    def land(self, j):
        return at(j * self.HALF, self.HALF)

    def c1(self, j):
        return copy(self.pc.at[self.other(j), :], self.rc1.at[self.slot(j), :],
                    self.s.at[0, j], self.v.at[0, j], self.r.sib)

    def c2(self, j):
        return copy(self.pc.at[self.mine(j), :], self.rc2.at[self.land(j), :],
                    self.s.at[1, j], self.v.at[1, j], self.r.ypeer)

    def c3(self, j):
        return copy(self.pc.at[self.mine(j), :], self.pc.at[self.mine(j), :],
                    self.s.at[2, j], self.v.at[2, j], self.r.sib)

    def y1(self, j):
        self.c1(j).start()

    def y2(self, j):
        self.c1(j).wait_recv()
        add_into(self.pc, self.mine(j), self.rc1, self.slot(j))
        self.c2(j).start()
        self.c1(j).wait_send()
        tell(self.free, self.r.sib)

    def y3(self, j, finish):
        self.c2(j).wait()
        add_into(self.pc, self.mine(j), self.rc2, self.land(j))
        pl.semaphore_wait(self.free, 1)
        self.c3(j).start()
        finish(j, self.r.core)

    def y4(self, j, finish):
        self.c3(j).wait()
        finish(j, 1 - self.r.core)


class GradSum:
    HALF = RC // 2

    def __init__(self, rank, g, ax, az, am, bz, bm, bx, a_s, a_r, b_s, b_r, free, na, nb):
        self.r, self.g = rank, g
        self.ax, self.az, self.am, self.bz, self.bm, self.bx = ax, az, am, bz, bm, bx
        self.a_s, self.a_r, self.b_s, self.b_r = a_s, a_r, b_s, b_r
        self.na, self.nb, self.free = na, nb, free

    def amine(self, k):
        return at(2 * k * RC + self.r.x * self.HALF, self.HALF)

    def aother(self, k):
        return at(2 * k * RC + (1 - self.r.x) * self.HALF, self.HALF)

    def buf(self, k):
        return at((k % RING) * self.HALF, self.HALF)

    def zbuf(self, k):
        return at((k % RING) * RC, RC)

    def ac(self, kind, k):
        g, m, b = self.g, self.amine(k), self.buf(k)
        src, dst, peer = (
            (g.at[self.aother(k), :], self.ax.at[b, :], self.r.xpeer),
            (g.at[m, :], self.az.at[b, :], self.r.zpeer),
            (g.at[m, :], self.am.at[b, :], self.r.mpeer),
            (g.at[m, :], g.at[m, :], self.r.zpeer),
            (g.at[m, :], g.at[m, :], self.r.xpeer),
        )[kind]
        return copy(src, dst, self.a_s.at[kind, k], self.a_r.at[kind, k], peer)

    def a1(self, k):
        self.ac(0, k).start()

    def a2(self, k):
        self.ac(0, k).wait_recv()
        add_into(self.g, self.amine(k), self.ax, self.buf(k))
        when(self.r.center == 0, lambda: self.ac(1, k).start())
        self.ac(0, k).wait_send()
        tell(self.free.at[0], self.r.xpeer)

    def a3(self, k):
        @pl.when(self.r.center == 1)
        def _():
            self.ac(1, k).wait_recv()
            add_into(self.g, self.amine(k), self.az, self.buf(k))
            self.ac(2, k).start()

        @pl.when(self.r.center == 0)
        def _():
            self.ac(1, k).wait_send()
            tell(self.free.at[1], self.r.zpeer)

    def a4(self, k):
        @pl.when(self.r.center == 1)
        def _():
            self.ac(2, k).wait()
            add_into(self.g, self.amine(k), self.am, self.buf(k))
            pl.semaphore_wait(self.free.at[1], 1)
            self.ac(3, k).start()
            pl.semaphore_wait(self.free.at[0], 1)
            self.ac(4, k).start()

    def a5(self, k):
        @pl.when(self.r.center == 0)
        def _():
            self.ac(3, k).wait_recv()
            pl.semaphore_wait(self.free.at[0], 1)
            self.ac(4, k).start()

    def a6(self, k):
        self.ac(4, k).wait()
        when(self.r.center == 1, lambda: self.ac(3, k).wait_send())

    def bfull(self, k):
        return at((2 * k + 1) * RC, RC)

    def bmine(self, k):
        return at((2 * k + 1) * RC + self.r.hm * self.HALF, self.HALF)

    def bother(self, k):
        return at((2 * k + 1) * RC + (1 - self.r.hm) * self.HALF, self.HALF)

    def bc(self, kind, k):
        g, f, m, o, b = self.g, self.bfull(k), self.bmine(k), self.bother(k), self.buf(k)
        src, dst, peer = (
            (g.at[f, :], self.bz.at[self.zbuf(k), :], self.r.zpeer),
            (g.at[o, :], self.bm.at[b, :], self.r.mpeer),
            (g.at[m, :], self.bx.at[b, :], self.r.xpeer),
            (g.at[m, :], g.at[m, :], self.r.mpeer),
            (g.at[m, :], g.at[m, :], self.r.zpeer),
            (g.at[o, :], g.at[o, :], self.r.zpeer),
        )[kind]
        return copy(src, dst, self.b_s.at[kind, k], self.b_r.at[kind, k], peer)

    def b1(self, k):
        when(self.r.center == 0, lambda: self.bc(0, k).start())

    def b2(self, k):
        @pl.when(self.r.center == 1)
        def _():
            self.bc(0, k).wait_recv()
            add_into(self.g, self.bfull(k), self.bz, self.zbuf(k))
            self.bc(1, k).start()

        @pl.when(self.r.center == 0)
        def _():
            self.bc(0, k).wait_send()
            tell(self.free.at[2], self.r.zpeer)

    def b3(self, k):
        @pl.when(self.r.center == 1)
        def _():
            self.bc(1, k).wait_recv()
            add_into(self.g, self.bmine(k), self.bm, self.buf(k))
            self.bc(2, k).start()
            self.bc(1, k).wait_send()
            tell(self.free.at[3], self.r.mpeer)

    def b4(self, k):
        @pl.when(self.r.center == 1)
        def _():
            self.bc(2, k).wait()
            add_into(self.g, self.bmine(k), self.bx, self.buf(k))
            pl.semaphore_wait(self.free.at[3], 1)
            self.bc(3, k).start()
            pl.semaphore_wait(self.free.at[2], 1)
            self.bc(4, k).start()

    def b5(self, k):
        @pl.when(self.r.center == 1)
        def _():
            self.bc(3, k).wait_recv()
            self.bc(5, k).start()

    def b6(self, k):
        @pl.when(self.r.center == 1)
        def _():
            self.bc(3, k).wait_send()
            self.bc(4, k).wait_send()
            self.bc(5, k).wait_send()

        @pl.when(self.r.center == 0)
        def _():
            self.bc(4, k).wait_recv()
            self.bc(5, k).wait_recv()

    def tick(self, t):
        for n, stages in ((self.nb, (self.b1, self.b2, self.b3, self.b4, self.b5, self.b6)),
                          (self.na, (self.a1, self.a2, self.a3, self.a4, self.a5, self.a6))):
            for back in range(5, -1, -1):
                k = t - back
                when(jnp.logical_and(k >= 0, k < n), lambda f=stages[back], k=k: f(k))


def block_kernel(
    grid, tokens_in, gain1_in, bias1_in, gain2_in, bias2_in, wqkvT_in, bqkv_in, wdense_in, wfc1_in,
    bfc1_in, wfc2_in, obias_in, cot_in, cosT_in, sinT_in,
    blk, gtok, g,
    tokens, wqkvT, bq, wdense, wfc1, wfc2, cot, cosT, sinT, gain1, bias1, gain2, bias2, bfc1, obias,
    bqkv, gpre, qT, kT, vT, gAT, qn, kn, vn, gAn, attT, dqT, dk, dv, gT, acc,
    pc, rc1, rc2, vs, vr1, vr2, ax, az, am, bz, bm, bx,
    i_s, y_s, y_r, v_s, v_r, a_s, a_r, b_s, b_r, y_f, d_f,
):
    n, D = tokens.shape
    seqs = n // LEN
    W = wdense.shape[0]
    F = wfc1.shape[1]
    heads = W // HD
    nblk = n // CH
    na, nb = a_s.shape[1], b_s.shape[1]
    r_fc2, r_fc1, r_qkv, r_dense, r_vec = 0, F, F + D, F + D + 3 * W, F + D + 4 * W
    hid2, act = blk, gtok
    hid1 = act

    part_rows = n // 4
    loads = [(tokens_in, tokens, 0)]
    loads += [(a, b, None) for a, b in (
        (gain2_in, gain2), (bias2_in, bias2), (wfc1_in, wfc1), (bfc1_in, bfc1), (wfc2_in, wfc2))]
    loads += [(cot_in, cot, 0)]
    loads += [(a, b, k) for k in range(1, 4) for a, b in ((tokens_in, tokens), (cot_in, cot))]
    early = len(loads)
    loads += [(a, b, None) for a, b in (
        (gain1_in, gain1), (bias1_in, bias1), (wqkvT_in, wqkvT), (bqkv_in, bq), (wdense_in, wdense),
        (cosT_in, cosT), (sinT_in, sinT), (obias_in, obias))]
    ins = []
    for i, (a, b, k) in enumerate(loads):
        if k is not None:
            a, b = a.at[pl.ds(k * part_rows, part_rows), :], b.at[pl.ds(k * part_rows, part_rows), :]
        ins.append(pltpu.make_async_copy(a, b, i_s.at[i]))
        ins[-1].start()

    rank = Ranks(grid)
    ts = TensorSum(rank, pc, rc1, rc2, y_s, y_r, y_f)
    gs = GradSum(rank, g, ax, az, am, bz, bm, bx, a_s, a_r, b_s, b_r, d_f, na, nb)

    def dp_tick(t):
        if grid:
            gs.tick(t)

    acc[...] = jnp.zeros_like(acc)
    g[at(r_qkv, g.shape[0] - r_qkv), :] = jnp.zeros((g.shape[0] - r_qkv, D), F32)

    for c in ins[:7]:
        c.wait()
    rank.barrier()

    def tile(i, carry):
        rows = at(i * TB, TB)
        xhat, _ = standardize(tokens[rows, :])
        h2 = (xhat * gain2[...][None, :] + bias2[...][None, :]).astype(BF)
        hid2[rows, :] = h2
        pre = nn(h2, wfc1[...]) + bfc1[...][None, :]
        cdf = 0.5 * (1.0 + lax.erf(pre * ROOT_HALF))
        a = (pre * cdf).astype(BF)
        act[rows, :] = a
        slope = cdf + pre * jnp.exp(-0.5 * pre * pre) * ROOT_TAU_INV
        ct = cot[rows, :]
        gp = (nt(ct, wfc2[...]) * slope).astype(BF)
        gpre[rows, :] = gp
        pc[rows, :] = nn(a, wfc2[...])
        g2 = nt(gp, wfc1[...])
        pc[at(n + i * TB, TB), :] = g2 * gain2[...][None, :]
        acc[2] += rowsum(g2 * xhat)
        acc[3] += rowsum(g2)
        acc[4] += rowsum(gp.astype(F32))
        acc[5] += rowsum(ct.astype(F32))
        return carry

    quarter = part_rows // TB
    lax.fori_loop(0, quarter, tile, 0)
    for c in ins[7:]:
        c.wait()
    lax.fori_loop(quarter, n // TB, tile, 0)
    for part in range(3):
        row = jnp.broadcast_to(bq[part : part + 1, :], (8, W))
        bqkv[part * W : (part + 1) * W, :] = row.T[:, 0:1]

    def wgrad(lhs, rhs, row):
        def body(j, carry):
            g[at(row + j * 256, 256), :] = tn(lhs[:, pl.ds(pl.multiple_of(j * 256, 256), 256)], rhs[...])
            return carry

        lax.fori_loop(0, lhs.shape[1] // 256, body, 0)

    wgrad(act, cot, r_fc2)

    def sentence(s, carry):
        base = s * LEN

        def proj(j, carry):
            cols = pl.ds(pl.multiple_of(j * QB, QB), QB)
            rows = at(base + j * QB, QB)
            c, sn = cosT[:, cols], sinT[:, cols]
            xhat, _ = standardize(tokens[rows, :])
            h1 = (xhat * gain1[...][None, :] + bias1[...][None, :]).astype(BF)
            hid1[rows, :] = h1
            pr = nt(wqkvT[...], h1) + bqkv[...]
            ga = nt(wdense[...], cot[rows, :]).astype(BF)
            gAT[:, cols] = ga
            for h in range(heads):
                for part, dT, dn in ((0, qT, qn), (1, kT, kn)):
                    o = part * W + h * HD
                    u, w = pr[o : o + 8], pr[o + 8 : o + 16]
                    full = jnp.concatenate(
                        [u * c - w * sn, w * c + u * sn, pr[o + 16 : o + HD]], 0
                    ).astype(BF)
                    dT[h * HD : (h + 1) * HD, cols] = full
                    dn[h, cols, :] = full.T
                o = 2 * W + h * HD
                vv = pr[o : o + HD].astype(BF)
                vT[h * HD : (h + 1) * HD, cols] = vv
                vn[h, cols, :] = vv.T
                gAn[h, cols, :] = ga[h * HD : (h + 1) * HD].T
            return carry

        dk[...] = jnp.zeros_like(dk)
        dv[...] = jnp.zeros_like(dv)
        for qb in range(LEN // QB):
            proj(qb, 0)
            nk = (qb + 1) * QB
            cols = slice(qb * QB, nk)

            mid, end = TICKS[qb]

            def head(h, carry):
                hr = pl.ds(pl.multiple_of(h * HD, HD), HD)
                st = nn(kn[h, :nk, :], qT[hr, cols])
                key = lax.broadcasted_iota(jnp.int32, (QB, QB), 0)
                qry = lax.broadcasted_iota(jnp.int32, (QB, QB), 1)
                diag = jnp.where(key <= qry, st[nk - QB :], -1e30)
                st = jnp.concatenate([st[: nk - QB], diag], 0) if nk > QB else diag
                top = jnp.max(st, 0, keepdims=True)
                e = jnp.exp2((st - top) * (SCALE * LOG2E))
                p = e * (1.0 / jnp.sum(e, 0, keepdims=True))
                low = p.astype(BF)
                attT[hr, cols] = nn(vT[hr, :nk], low).astype(BF)
                gp = nn(vn[h, :nk, :], gAT[hr, cols])
                inner = jnp.sum(p * gp, 0, keepdims=True)
                ds = (p * (gp - inner)).astype(BF)
                dqT[hr, cols] = nn(kT[hr, :nk], ds) * SCALE
                dk[h, :nk, :] += nn(ds, qn[h, cols, :])
                dv[h, :nk, :] += nn(low, gAn[h, cols, :])
                if mid is not None:
                    when(h == 1, lambda: dp_tick(s * PER + mid))
                return carry

            lax.fori_loop(0, heads, head, 0)
            pc[at(base + qb * QB, QB), :] += tn(attT[:, cols], wdense[...])
            j = s * (LEN // QB) + qb
            ts.y1(j)
            if qb == 0:
                when(s == 0, lambda: wgrad(hid2, gpre, r_fc1))
            dp_tick(s * PER + end)
            ts.y2(j)

        def back(j, carry):
            cols = pl.ds(pl.multiple_of(j * QB, QB), QB)
            rows = at(base + j * QB, QB)
            c, sn = cosT[:, cols], sinT[:, cols]
            for h in range(heads):
                hs = slice(h * HD, (h + 1) * HD)
                for k, gr in ((0, dqT[hs, cols]), (1, dk[h, cols, :].T * SCALE)):
                    u, w = gr[0:8], gr[8:16]
                    gT[k * W + h * HD : k * W + (h + 1) * HD, cols] = jnp.concatenate(
                        [u * c + w * sn, w * c - u * sn, gr[16:]], 0
                    ).astype(BF)
                gT[2 * W + h * HD : 2 * W + (h + 1) * HD, cols] = dv[h, cols, :].T.astype(BF)
            g1 = tn(gT[:, cols], wqkvT[...])
            xhat, _ = standardize(tokens[rows, :])
            pc[at(n + base + j * QB, QB), :] += g1 * gain1[...][None, :]
            acc[0] += rowsum(g1 * xhat)
            acc[1] += rowsum(g1)
            return carry

        lax.fori_loop(0, LEN // QB, back, 0)
        srows = at(base, LEN)
        g[at(r_qkv, 3 * W), :] += nn(gT[...], hid1[srows, :])
        g[at(r_dense, W), :] += nn(attT[...], cot[srows, :])
        ones = jnp.ones((8, LEN), BF)
        g[r_vec + 6 : r_vec + 7, 0 : 3 * W] += nt(ones, gT[...])[0:1]
        dp_tick(s * PER + PER - 1)
        return carry

    lax.fori_loop(0, seqs, sentence, 0)

    vs[...] = jnp.sum(acc[...], 1)
    v1 = copy(vs, vr1, v_s.at[0], v_r.at[0], rank.sib)
    v1.start()
    g[r_vec + 4 : r_vec + 6, :] = vs[4:6, :]
    v1.wait()
    vs[...] = vs[...] + vr1[...]
    v2 = copy(vs, vr2, v_s.at[1], v_r.at[1], rank.ypeer)
    v2.start()
    v2.wait()
    g[r_vec : r_vec + 4, :] = vs[0:4, :] + vr2[0:4, :]

    def finish_block(j, half):
        rows = at(j * CH + half * (CH // 2), CH // 2)
        blk[rows, :] = (tokens[rows, :].astype(F32) + pc[rows, :] + obias[...][None, :]).astype(BF)

    def finish_tokens(j, half):
        rows = at((j - nblk) * CH + half * (CH // 2), CH // 2)
        c = pc[at(j * CH + half * (CH // 2), CH // 2), :]
        xhat, inv = standardize(tokens[rows, :])
        inside = c - jnp.mean(c, -1, keepdims=True) - xhat * jnp.mean(c * xhat, -1, keepdims=True)
        gtok[rows, :] = (cot[rows, :].astype(F32) + inv * inside).astype(BF)

    LEAD = 8

    def drain(u, carry):
        when(jnp.logical_and(u >= 1, u <= nblk), lambda: ts.y4(u - 1, finish_block))
        when(jnp.logical_and(u > nblk, u <= 2 * nblk), lambda: ts.y4(u - 1, finish_tokens))
        when(u < nblk, lambda: ts.y3(u, finish_block))
        when(jnp.logical_and(u >= nblk, u < 2 * nblk), lambda: ts.y3(u, finish_tokens))
        when(jnp.logical_and(u + LEAD - 1 >= nblk, u + LEAD - 1 < 2 * nblk), lambda: ts.y2(u + LEAD - 1))
        when(jnp.logical_and(u + LEAD >= nblk, u + LEAD < 2 * nblk), lambda: ts.y1(u + LEAD))
        dp_tick(seqs * PER + 2 * u)
        dp_tick(seqs * PER + 2 * u + 1)
        return carry

    last = max(na, nb) + 5 - seqs * PER
    steps = max(2 * nblk + 1, (last + 1) // 2 if grid else 0)
    lax.fori_loop(0, steps, drain, 0)


def tail_kernel(
    blk, gtok, g, blk_out, gtok_out, gfc2, gfc1, gqkv, gdense, v0, v1, v2, v3, v4, v5, gb, sems
):
    F, D, W = gfc2.shape[0], gfc1.shape[0], gdense.shape[0]
    copies = []

    def out(src, dst):
        for k in range(2):
            rows = pl.ds(k * (dst.shape[0] // 2), dst.shape[0] // 2)
            copies.append(pltpu.make_async_copy(src.at[rows, :], dst.at[rows, :], sems.at[len(copies)]))
            copies[-1].start()

    out(blk, blk_out)
    out(gtok, gtok_out)
    out(g.at[0:F, :], gfc2)
    out(g.at[F : F + D, :], gfc1)
    out(g.at[F + D : F + D + 3 * W, :], gqkv)
    out(g.at[F + D + 3 * W : F + D + 4 * W, :], gdense)
    at_vec = F + D + 4 * W
    for i, v in enumerate((v0, v1, v2, v3, v4, v5)):
        v[...] = g[at_vec + i]
    for c in range(3):
        gb[c : c + 1, :] = g[at_vec + 6 : at_vec + 7, c * W : (c + 1) * W]
    for c in copies:
        c.wait()


def tail(blk, gtok, g, F, W):
    n, D = blk.shape
    sd = jax.ShapeDtypeStruct
    here, there = pl.BlockSpec(memory_space=VMEM), pl.BlockSpec(memory_space=pl.ANY)
    return pl.pallas_call(
        tail_kernel,
        out_shape=(
            sd((n, D), BF), sd((n, D), BF), sd((F, D), F32), sd((D, F), F32), sd((3 * W, D), F32),
            sd((W, D), F32), *([sd((D,), F32)] * 6), sd((3, W), F32),
        ),
        in_specs=[here] * 3,
        out_specs=[there] * 6 + [here] * 7,
        scratch_shapes=[pltpu.SemaphoreType.DMA((12,))],
        compiler_params=pltpu.CompilerParams(vmem_limit_bytes=2**20),
        name="tail",
    )(blk, gtok, g)


def block(grid, tokens, vectors, wqkvT, bqkv, wdense, wfc1, wfc2, cot):
    n, D = tokens.shape
    W = wdense.shape[0]
    heads = W // HD
    F = wfc1.shape[1]
    angle = np.arange(LEN, dtype=np.float64)[None, :] / 10000.0 ** (
        np.arange(0, ROT, 2, dtype=np.float64)[:, None] / ROT
    )
    cosT = jnp.asarray(np.cos(angle), F32)
    sinT = jnp.asarray(np.sin(angle), F32)
    g1, b1, g2, b2, bfc1, ob = vectors
    pairs = (F + D + 4 * W) // (2 * RC)
    na, nb = pairs + 1, pairs
    rows = (na + nb) * RC
    half, DMA = RC // 2, pltpu.SemaphoreType.DMA
    sd = jax.ShapeDtypeStruct
    inputs = (tokens, g1, b1, g2, b2, wqkvT, bqkv, wdense, wfc1, bfc1, wfc2, ob, cot, cosT, sinT)
    nch = 2 * n // CH
    return pl.pallas_call(
        lambda *refs: block_kernel(grid, *refs),
        out_shape=(VMEM((n, D), BF), VMEM((n, D), BF), VMEM((rows, D), F32)),
        in_specs=[pl.BlockSpec(memory_space=pl.ANY)] * len(inputs),
        out_specs=[pl.BlockSpec(memory_space=VMEM)] * 3,
        scratch_shapes=[
            VMEM((n, D), BF), VMEM((3 * W, D), BF), VMEM((3, W), F32), VMEM((W, D), BF),
            VMEM((D, F), BF), VMEM((F, D), BF), VMEM((n, D), BF),
            VMEM((ROT // 2, LEN), F32), VMEM((ROT // 2, LEN), F32), *([VMEM((D,), F32)] * 4),
            VMEM((F,), F32), VMEM((D,), F32), VMEM((3 * W, 1), F32),
            VMEM((n, F), BF),
            VMEM((W, LEN), BF), VMEM((W, LEN), BF), VMEM((W, LEN), BF), VMEM((W, LEN), BF),
            VMEM((heads, LEN, HD), BF), VMEM((heads, LEN, HD), BF),
            VMEM((heads, LEN, HD), BF), VMEM((heads, LEN, HD), BF),
            VMEM((W, LEN), BF), VMEM((W, LEN), F32),
            VMEM((heads, LEN, HD), F32), VMEM((heads, LEN, HD), F32),
            VMEM((3 * W, LEN), BF), VMEM((8, 8, D), F32),
            VMEM((2 * n, D), F32),
            VMEM((SLOTS * CH // 2, D), F32), VMEM((nch * CH // 2, D), F32),
            VMEM((8, D), F32), VMEM((8, D), F32), VMEM((8, D), F32),
            VMEM((RING * half, D), F32), VMEM((RING * half, D), F32), VMEM((RING * half, D), F32),
            VMEM((RING * RC, D), F32), VMEM((RING * half, D), F32), VMEM((RING * half, D), F32),
            DMA((24,)), DMA((3, nch)), DMA((3, nch)), DMA((2,)), DMA((2,)),
            DMA((5, na)), DMA((5, na)), DMA((6, nb)), DMA((6, nb)),
            pltpu.SemaphoreType.REGULAR, pltpu.SemaphoreType.REGULAR((4,)),
        ],
        compiler_params=pltpu.CompilerParams(
            vmem_limit_bytes=SCOPED, collective_id=0, has_side_effects=True
        ),
        name="block",
    )(*inputs)


def on_device(
    grid, tokens, attention_norm_gain, attention_norm_bias, feedforward_norm_gain,
    feedforward_norm_bias, w_qkv, b_qkv, w_dense, w_fc1, b_fc1, w_fc2, out_bias, cotangent,
):
    D = tokens.shape[1]
    W, F = w_dense.shape[0], w_fc1.shape[1]
    wqkvT = jnp.transpose(w_qkv, (1, 2, 0)).reshape(3 * W, D)
    vectors = (
        attention_norm_gain, attention_norm_bias, feedforward_norm_gain, feedforward_norm_bias,
        b_fc1, out_bias,
    )
    block_out, grad_tokens, grads = block(
        grid, tokens, vectors, wqkvT, b_qkv, w_dense, w_fc1, w_fc2, cotangent
    )
    if not grid:
        grads = lax.psum(grads, "dp")
    blk, gtok, gfc2, gfc1, gqkvT, gdense, v0, v1, v2, v3, v4, v5, gb = tail(
        block_out, grad_tokens, grads, F, W
    )
    gqkv = jnp.transpose(gqkvT.reshape(3, W, D), (2, 0, 1))
    return (blk, gtok, v0, v1, v2, v3, gqkv, gb, gdense, gfc1, v4, gfc2, v5)


def solution(mesh):
    placed = (
        P("dp", None), P(), P(), P(), P(), P(None, None, "tensor"), P(None, "tensor"),
        P("tensor", None), P(None, "tensor"), P("tensor"), P("tensor", None), P(), P("dp", None),
    )
    grid = mesh.shape["dp"] == 8
    return jax.shard_map(
        lambda *args: on_device(grid, *args), mesh=mesh, in_specs=placed,
        out_specs=(
            P("dp", None), P("dp", None), P(), P(), P(), P(), P(None, None, "tensor"),
            P(None, "tensor"), P("tensor", None), P(None, "tensor"), P("tensor"),
            P("tensor", None), P(),
        ),
        check_vma=False,
    )
```

```python
import math

import jax
import jax.numpy as jnp
import numpy as np
from jax import lax
from jax.experimental import pallas as pl
from jax.experimental.pallas import tpu as pltpu
from jax.sharding import PartitionSpec as P

HD = 64
ROT = 16
LEN = 1024
QB = 256
TB = 256
CH = 256
RC = 48
LANDS = 12
SLOTS = 4
RING = 8
SEMS = 11
LAG = 2
SCOPED = 50 * 2**20
TICKS = ((None, 0), (None, 1), (2, 3), (4, 5))
PER = 7
LEAD = 4
FAR = 2
MESH = pl.DeviceIdType.MESH
BF = jnp.bfloat16
F32 = jnp.float32
ROOT_HALF = 0.7071067811865476
ROOT_TAU_INV = 0.3989422804014327
LOG2E = 1.4426950408889634
SCALE = HD ** (-0.5)
VMEM = pltpu.VMEM


def nn(a, b):
    return lax.dot_general(a, b, (((1,), (0,)), ((), ())), preferred_element_type=F32)


def nt(a, b):
    return lax.dot_general(a, b, (((1,), (1,)), ((), ())), preferred_element_type=F32)


def tn(a, b):
    return lax.dot_general(a, b, (((0,), (0,)), ((), ())), preferred_element_type=F32)


def rowsum(v):
    return jnp.sum(v.reshape(v.shape[0] // 8, 8, v.shape[1]), 0)


def standardize(rows):
    x = rows.astype(F32)
    centered = x - jnp.mean(x, -1, keepdims=True)
    inv = lax.rsqrt(jnp.mean(centered * centered, -1, keepdims=True) + 1e-5)
    return centered * inv, inv


def when(cond, f):
    pl.when(cond)(f)


class Ranks:
    def __init__(self, grid):
        t = lax.axis_index("tensor")
        d = lax.axis_index("dp")
        self.core = t % 2
        self.sib = {"tensor": t + 1 - 2 * (t % 2)}
        self.ypeer = {"tensor": (t + 2) % 4}
        self.x = d % 2
        z = d // 2
        self.xpeer = {"dp": d + 1 - 2 * (d % 2)}
        self.zpeer = {"dp": d + 2 - 4 * (z % 2)}
        self.mpeer = {"dp": (3 - z) * 2 + d % 2}
        self.center = ((z + 1) // 2) % 2
        self.hm = (z // 2) % 2
        self.grid = grid

    def greet(self):
        peers = [self.sib, self.ypeer]
        if self.grid:
            peers += [self.xpeer, self.zpeer, self.mpeer]
        sem = pltpu.get_barrier_semaphore()
        for peer in peers:
            pl.semaphore_signal(sem, inc=1, device_id=peer, device_id_type=MESH)
        return lambda: pl.semaphore_wait(sem, len(peers))


def at(start, size):
    return pl.ds(pl.multiple_of(start, 8), size)


def copy(src, dst, send, recv, peer):
    return pltpu.make_async_remote_copy(
        src_ref=src, dst_ref=dst, send_sem=send, recv_sem=recv, device_id=peer,
        device_id_type=MESH,
    )


def tell(sem, peer):
    pl.semaphore_signal(sem, inc=1, device_id=peer, device_id_type=MESH)


def add_into(dst, rows, src, srows):
    dst[rows, :] = dst[rows, :] + src[srows, :]


class TensorSum:
    HALF = CH // 2

    def __init__(self, rank, pc, rc1, rc2, send, recv, free):
        self.r, self.pc, self.rc1, self.rc2 = rank, pc, rc1, rc2
        self.s, self.v, self.free = send, recv, free
        self.n = pc.shape[0] // CH

    def mine(self, j):
        return at(j * CH + self.r.core * self.HALF, self.HALF)

    def other(self, j):
        return at(j * CH + (1 - self.r.core) * self.HALF, self.HALF)

    def slot(self, j):
        return at((j % SLOTS) * self.HALF, self.HALF)

    def land(self, j):
        return at((j % LANDS) * self.HALF, self.HALF)

    def c1(self, j):
        return copy(self.pc.at[self.other(j), :], self.rc1.at[self.slot(j), :],
                    self.s.at[2, j % SLOTS], self.v.at[2, j % SLOTS], self.r.sib)

    def c2(self, j):
        return copy(self.pc.at[self.mine(j), :], self.rc2.at[self.land(j), :],
                    self.s.at[0, j], self.v.at[0, j], self.r.ypeer)

    def c3(self, j):
        return copy(self.pc.at[self.mine(j), :], self.pc.at[self.mine(j), :],
                    self.s.at[1, j], self.v.at[1, j], self.r.sib)

    def y1(self, j):
        when(j >= SLOTS, lambda: pl.semaphore_wait(self.free, 1))
        self.c1(j).start()

    def y2(self, j):
        self.c1(j).wait_recv()
        add_into(self.pc, self.mine(j), self.rc1, self.slot(j))
        self.c2(j).start()
        self.c1(j).wait_send()
        tell(self.free, self.r.sib)

    def y3(self, j, finish):
        self.c2(j).wait()
        add_into(self.pc, self.mine(j), self.rc2, self.land(j))
        when(j >= self.n - SLOTS, lambda: pl.semaphore_wait(self.free, 1))
        self.c3(j).start()
        finish(j, self.r.core)

    def y4(self, j, finish):
        self.c3(j).wait()
        finish(j, 1 - self.r.core)


class GradSum:
    HALF = RC // 2

    def __init__(self, rank, g, ax, az, am, bz, bm, bx, a_s, a_r, b_s, b_r, free, na, nb):
        self.r, self.g = rank, g
        self.ax, self.az, self.am, self.bz, self.bm, self.bx = ax, az, am, bz, bm, bx
        self.a_s, self.a_r, self.b_s, self.b_r = a_s, a_r, b_s, b_r
        self.na, self.nb, self.free = na, nb, free

    def amine(self, k):
        return at(2 * k * RC + self.r.x * self.HALF, self.HALF)

    def aother(self, k):
        return at(2 * k * RC + (1 - self.r.x) * self.HALF, self.HALF)

    def buf(self, k):
        return at((k % RING) * self.HALF, self.HALF)

    def zbuf(self, k):
        return at((k % RING) * RC, RC)

    def ac(self, kind, k):
        g, m, b = self.g, self.amine(k), self.buf(k)
        src, dst, peer = (
            (g.at[self.aother(k), :], self.ax.at[b, :], self.r.xpeer),
            (g.at[m, :], self.az.at[b, :], self.r.zpeer),
            (g.at[m, :], self.am.at[b, :], self.r.mpeer),
            (g.at[m, :], g.at[m, :], self.r.zpeer),
            (g.at[m, :], g.at[m, :], self.r.xpeer),
        )[kind]
        return copy(src, dst, self.a_s.at[kind, k % SEMS], self.a_r.at[kind, k % SEMS], peer)

    def a1(self, k):
        self.ac(0, k).start()

    def a2(self, k):
        self.ac(0, k).wait_recv()
        add_into(self.g, self.amine(k), self.ax, self.buf(k))
        when(self.r.center == 0, lambda: self.ac(1, k).start())
        self.ac(0, k).wait_send()
        tell(self.free.at[0], self.r.xpeer)

    def a3(self, k):
        @pl.when(self.r.center == 1)
        def _():
            self.ac(1, k).wait_recv()
            add_into(self.g, self.amine(k), self.az, self.buf(k))
            self.ac(2, k).start()

        @pl.when(self.r.center == 0)
        def _():
            self.ac(1, k).wait_send()
            tell(self.free.at[1], self.r.zpeer)

    def a4(self, k):
        @pl.when(self.r.center == 1)
        def _():
            self.ac(2, k).wait()
            add_into(self.g, self.amine(k), self.am, self.buf(k))
            pl.semaphore_wait(self.free.at[1], 1)
            self.ac(3, k).start()
            pl.semaphore_wait(self.free.at[0], 1)
            self.ac(4, k).start()

    def a5(self, k):
        @pl.when(self.r.center == 0)
        def _():
            self.ac(3, k).wait_recv()
            pl.semaphore_wait(self.free.at[0], 1)
            self.ac(4, k).start()

    def a6(self, k):
        self.ac(4, k).wait()
        when(self.r.center == 1, lambda: self.ac(3, k).wait_send())

    def bfull(self, k):
        return at((2 * k + 1) * RC, RC)

    def bmine(self, k):
        return at((2 * k + 1) * RC + self.r.hm * self.HALF, self.HALF)

    def bother(self, k):
        return at((2 * k + 1) * RC + (1 - self.r.hm) * self.HALF, self.HALF)

    def bc(self, kind, k):
        g, f, m, o, b = self.g, self.bfull(k), self.bmine(k), self.bother(k), self.buf(k)
        src, dst, peer = (
            (g.at[f, :], self.bz.at[self.zbuf(k), :], self.r.zpeer),
            (g.at[o, :], self.bm.at[b, :], self.r.mpeer),
            (g.at[m, :], self.bx.at[b, :], self.r.xpeer),
            (g.at[m, :], g.at[m, :], self.r.mpeer),
            (g.at[m, :], g.at[m, :], self.r.zpeer),
            (g.at[o, :], g.at[o, :], self.r.zpeer),
        )[kind]
        return copy(src, dst, self.b_s.at[kind, k % SEMS], self.b_r.at[kind, k % SEMS], peer)

    def b1(self, k):
        when(self.r.center == 0, lambda: self.bc(0, k).start())

    def b2(self, k):
        @pl.when(self.r.center == 1)
        def _():
            self.bc(0, k).wait_recv()
            add_into(self.g, self.bfull(k), self.bz, self.zbuf(k))
            self.bc(1, k).start()

        @pl.when(self.r.center == 0)
        def _():
            self.bc(0, k).wait_send()
            tell(self.free.at[2], self.r.zpeer)

    def b3(self, k):
        @pl.when(self.r.center == 1)
        def _():
            self.bc(1, k).wait_recv()
            add_into(self.g, self.bmine(k), self.bm, self.buf(k))
            self.bc(2, k).start()
            self.bc(1, k).wait_send()
            tell(self.free.at[3], self.r.mpeer)

    def b4(self, k):
        @pl.when(self.r.center == 1)
        def _():
            self.bc(2, k).wait()
            add_into(self.g, self.bmine(k), self.bx, self.buf(k))
            pl.semaphore_wait(self.free.at[3], 1)
            self.bc(3, k).start()
            pl.semaphore_wait(self.free.at[2], 1)
            self.bc(4, k).start()

    def b5(self, k):
        @pl.when(self.r.center == 1)
        def _():
            self.bc(3, k).wait_recv()
            self.bc(5, k).start()

    def b6(self, k):
        @pl.when(self.r.center == 1)
        def _():
            self.bc(3, k).wait_send()
            self.bc(4, k).wait_send()
            self.bc(5, k).wait_send()

        @pl.when(self.r.center == 0)
        def _():
            self.bc(4, k).wait_recv()
            self.bc(5, k).wait_recv()

    def tick(self, t):
        for n, stages in ((self.na, (self.a1, self.a2, self.a3, self.a4, self.a5, self.a6)),
                          (self.nb, (self.b1, self.b2, self.b3, self.b4, self.b5, self.b6))):
            for back in range(5, -1, -1):
                k = t - LAG * back
                when(jnp.logical_and(k >= 0, k < n), lambda f=stages[back], k=k: f(k))


def block_kernel(
    grid, tokens_in, gain1_in, bias1_in, gain2_in, bias2_in, wqkvT_in, bqkv_in, wdense_in, wfc1_in,
    bfc1_in, wfc2_in, obias_in, cot_in, cosT_in, sinT_in,
    blk, gtok, g,
    tokens, wqkvT, bq, wdense, wfc1, wfc2, cot, cosT, sinT, gain1, bias1, gain2, bias2, bfc1, obias,
    bqkv, stash, gpre, qT, kT, vT, gAT, qn, kn, vn, gAn, attT, dqT, dk, dv, gT, acc,
    pc, rc1, rc2, vs, vr1, vr2, ax, az, am, bz, bm, bx,
    i_s, y_s, y_r, v_s, v_r, a_s, a_r, b_s, b_r, y_f, d_f,
):
    n, D = tokens.shape
    seqs = n // LEN
    W = wdense.shape[0]
    F = wfc1.shape[1]
    heads = W // HD
    nblk = n // CH
    pairs = (F + D + 4 * W) // (2 * RC)
    na, nb = pairs + 1, pairs
    r_fc2, r_fc1, r_qkv, r_dense, r_vec = 0, F, F + D, F + D + 3 * W, F + D + 4 * W
    hid2, act = blk, gtok
    hid1 = act

    part_rows = n // 4
    loads = [(tokens_in, tokens, 0)]
    loads += [(a, b, None) for a, b in (
        (gain2_in, gain2), (bias2_in, bias2), (wfc1_in, wfc1), (bfc1_in, bfc1), (wfc2_in, wfc2))]
    loads += [(cot_in, cot, 0)]
    loads += [(a, b, k) for k in range(1, 4) for a, b in ((tokens_in, tokens), (cot_in, cot))]
    early = len(loads)
    loads += [(a, b, None) for a, b in (
        (gain1_in, gain1), (bias1_in, bias1), (wqkvT_in, wqkvT), (bqkv_in, bq), (wdense_in, wdense),
        (cosT_in, cosT), (sinT_in, sinT), (obias_in, obias))]
    ins = []
    for i, (a, b, k) in enumerate(loads):
        if k is not None:
            a, b = a.at[pl.ds(k * part_rows, part_rows), :], b.at[pl.ds(k * part_rows, part_rows), :]
        ins.append(pltpu.make_async_copy(a, b, i_s.at[i]))
        ins[-1].start()

    rank = Ranks(grid)
    all_here = rank.greet()
    ts = TensorSum(rank, pc, rc1, rc2, y_s, y_r, y_f)
    gs = GradSum(rank, g, ax, az, am, bz, bm, bx, a_s, a_r, b_s, b_r, d_f, na, nb)

    def dp_tick(t):
        if grid:
            gs.tick(t)

    acc[...] = jnp.zeros_like(acc)
    g[at(r_qkv, g.shape[0] - r_qkv), :] = jnp.zeros((g.shape[0] - r_qkv, D), F32)

    for c in ins[:7]:
        c.wait()

    def tile(i, carry):
        rows = at(i * TB, TB)
        xhat, _ = standardize(tokens[rows, :])
        h2 = (xhat * gain2[...][None, :] + bias2[...][None, :]).astype(BF)
        hid2[rows, :] = h2
        pre = nn(h2, wfc1[...]) + bfc1[...][None, :]
        cdf = 0.5 * (1.0 + lax.erf(pre * ROOT_HALF))
        a = (pre * cdf).astype(BF)
        act[rows, :] = a
        slope = cdf + pre * jnp.exp(-0.5 * pre * pre) * ROOT_TAU_INV
        ct = cot[rows, :]
        gp = (nt(ct, wfc2[...]) * slope).astype(BF)
        gpre[rows, :] = gp
        out = at(i * TB + (i // (LEN // TB)) * LEN, TB)
        pc[out, :] = nn(a, wfc2[...])
        g2 = nt(gp, wfc1[...])
        pc[at((i // (LEN // TB) + 1) * LEN + i * TB, TB), :] = g2 * gain2[...][None, :]
        acc[2] += rowsum(g2 * xhat)
        acc[3] += rowsum(g2)
        acc[4] += rowsum(gp.astype(F32))
        acc[5] += rowsum(ct.astype(F32))
        return carry

    quarter = part_rows // TB
    lax.fori_loop(0, quarter, tile, 0)
    for c in ins[7:]:
        c.wait()
    lax.fori_loop(quarter, n // TB, tile, 0)
    for part in range(3):
        row = jnp.broadcast_to(bq[part : part + 1, :], (8, W))
        bqkv[part * W : (part + 1) * W, :] = row.T[:, 0:1]

    def wgrad(lhs, rhs, row, first=0, last=None):
        def body(j, carry):
            g[at(row + j * 256, 256), :] = tn(lhs[:, pl.ds(pl.multiple_of(j * 256, 256), 256)], rhs[...])
            return carry

        lax.fori_loop(first, last or lhs.shape[1] // 256, body, 0)

    all_here()

    quarter = LEN // CH

    def finish_block(j, half):
        rows = at((j // (2 * quarter)) * LEN + (j % quarter) * CH + half * (CH // 2), CH // 2)
        summed = pc[at(j * CH + half * (CH // 2), CH // 2), :]
        blk[rows, :] = (tokens[rows, :].astype(F32) + summed + obias[...][None, :]).astype(BF)

    def finish_tokens(j, half):
        rows = at((j // (2 * quarter)) * LEN + (j % quarter) * CH + half * (CH // 2), CH // 2)
        c = pc[at(j * CH + half * (CH // 2), CH // 2), :]
        xhat, inv = standardize(tokens[rows, :])
        inside = c - jnp.mean(c, -1, keepdims=True) - xhat * jnp.mean(c * xhat, -1, keepdims=True)
        gtok[rows, :] = (cot[rows, :].astype(F32) + inv * inside).astype(BF)

    def finish(j, half):
        is_block = (j // quarter) % 2 == 0
        when(is_block, lambda: finish_block(j, half))
        when(jnp.logical_not(is_block), lambda: finish_tokens(j, half))

    def sentence(s, carry):
        base = s * LEN

        def proj(j, carry):
            cols = pl.ds(pl.multiple_of(j * QB, QB), QB)
            rows = at(base + j * QB, QB)
            c, sn = cosT[:, cols], sinT[:, cols]
            xhat, _ = standardize(tokens[rows, :])
            h1 = (xhat * gain1[...][None, :] + bias1[...][None, :]).astype(BF)
            if j == 0:
                stash[...] = h1
            else:
                hid1[rows, :] = h1
            pr = nt(wqkvT[...], h1) + bqkv[...]
            ga = nt(wdense[...], cot[rows, :]).astype(BF)
            gAT[:, cols] = ga
            for h in range(heads):
                for part, dT, dn in ((0, qT, qn), (1, kT, kn)):
                    o = part * W + h * HD
                    u, w = pr[o : o + 8], pr[o + 8 : o + 16]
                    full = jnp.concatenate(
                        [u * c - w * sn, w * c + u * sn, pr[o + 16 : o + HD]], 0
                    ).astype(BF)
                    dT[h * HD : (h + 1) * HD, cols] = full
                    dn[h, cols, :] = full.T
                o = 2 * W + h * HD
                vv = pr[o : o + HD].astype(BF)
                vT[h * HD : (h + 1) * HD, cols] = vv
                vn[h, cols, :] = vv.T
                gAn[h, cols, :] = ga[h * HD : (h + 1) * HD].T
            return carry

        dk[...] = jnp.zeros_like(dk)
        dv[...] = jnp.zeros_like(dv)
        for qb in range(LEN // QB):
            proj(qb, 0)
            nk = (qb + 1) * QB
            cols = slice(qb * QB, nk)

            mid, end = TICKS[qb]

            def head(h, carry):
                hr = pl.ds(pl.multiple_of(h * HD, HD), HD)
                st = nn(kn[h, :nk, :], qT[hr, cols])
                key = lax.broadcasted_iota(jnp.int32, (QB, QB), 0)
                qry = lax.broadcasted_iota(jnp.int32, (QB, QB), 1)
                diag = jnp.where(key <= qry, st[nk - QB :], -1e30)
                st = jnp.concatenate([st[: nk - QB], diag], 0) if nk > QB else diag
                top = jnp.max(st, 0, keepdims=True)
                e = jnp.exp2((st - top) * (SCALE * LOG2E))
                p = e * (1.0 / jnp.sum(e, 0, keepdims=True))
                low = p.astype(BF)
                attT[hr, cols] = nn(vT[hr, :nk], low).astype(BF)
                gp = nn(vn[h, :nk, :], gAT[hr, cols])
                inner = jnp.sum(p * gp, 0, keepdims=True)
                ds = (p * (gp - inner)).astype(BF)
                dqT[hr, cols] = nn(kT[hr, :nk], ds) * SCALE
                dk[h, :nk, :] += nn(ds, qn[h, cols, :])
                dv[h, :nk, :] += nn(low, gAn[h, cols, :])
                if mid is not None:
                    when(h == 1, lambda: dp_tick(s * PER + mid))
                return carry

            lax.fori_loop(0, heads, head, 0)
            pc[at(2 * base + qb * QB, QB), :] += tn(attT[:, cols], wdense[...])
            j = s * (LEN // QB) + qb
            ts.y1(j)
            if qb == 0:
                when(s == 0, lambda: wgrad(act, cot, r_fc2, 0, 2))
                dp_tick(s * PER + end)
                ts.y2(j)
                when(s == 0, lambda: wgrad(act, cot, r_fc2, 2))
                hid1[at(base, QB), :] = stash[...]
            else:
                dp_tick(s * PER + end)
                ts.y2(j)
            if qb == 1:
                when(s == 0, lambda: wgrad(hid2, gpre, r_fc1))

            @pl.when(s > 0)
            def _():
                if qb > 0:
                    ts.y4(qb - 1, finish)
                ts.y3(qb, finish)

        def back(j, carry):
            cols = pl.ds(pl.multiple_of(j * QB, QB), QB)
            rows = at(base + j * QB, QB)
            c, sn = cosT[:, cols], sinT[:, cols]
            for h in range(heads):
                hs = slice(h * HD, (h + 1) * HD)
                for k, gr in ((0, dqT[hs, cols]), (1, dk[h, cols, :].T * SCALE)):
                    u, w = gr[0:8], gr[8:16]
                    gT[k * W + h * HD : k * W + (h + 1) * HD, cols] = jnp.concatenate(
                        [u * c + w * sn, w * c - u * sn, gr[16:]], 0
                    ).astype(BF)
                gT[2 * W + h * HD : 2 * W + (h + 1) * HD, cols] = dv[h, cols, :].T.astype(BF)
            g1 = tn(gT[:, cols], wqkvT[...])
            xhat, _ = standardize(tokens[rows, :])
            pc[at(2 * base + LEN + j * QB, QB), :] += g1 * gain1[...][None, :]
            acc[0] += rowsum(g1 * xhat)
            acc[1] += rowsum(g1)
            return carry

        lax.fori_loop(0, LEN // QB, back, 0)
        srows = at(base, LEN)
        g[at(r_qkv, 3 * W), :] += nn(gT[...], hid1[srows, :])
        g[at(r_dense, W), :] += nn(attT[...], cot[srows, :])
        ones = jnp.ones((8, LEN), BF)
        g[r_vec + 6 : r_vec + 7, 0 : 3 * W] += nt(ones, gT[...])[0:1]
        dp_tick(s * PER + PER - 1)
        return carry

    lax.fori_loop(0, seqs, sentence, 0)

    def chunk_step(u, carry):
        when(jnp.logical_and(u >= 1, u <= 2 * nblk), lambda: ts.y4(u - 1, finish))
        when(jnp.logical_and(u + LEAD >= nblk, u + LEAD < 2 * nblk), lambda: ts.y1(u + LEAD))
        when(u < 2 * nblk, lambda: ts.y3(u, finish))
        when(jnp.logical_and(u + LEAD - 1 >= nblk, u + LEAD - 1 < 2 * nblk), lambda: ts.y2(u + LEAD - 1))
        return carry

    vs[...] = jnp.sum(acc[...], 1)
    g[r_vec + 4 : r_vec + 6, :] = vs[4:6, :]
    v1 = copy(vs, vr1, v_s.at[0], v_r.at[0], rank.sib)
    v1.start()
    lax.fori_loop(quarter, quarter + 2, chunk_step, 0)
    v1.wait()
    vs[...] = vs[...] + vr1[...]
    v2 = copy(vs, vr2, v_s.at[1], v_r.at[1], rank.ypeer)
    v2.start()
    lax.fori_loop(quarter + 2, quarter + 3, chunk_step, 0)
    v2.wait()
    g[r_vec : r_vec + 4, :] = vs[0:4, :] + vr2[0:4, :]

    def drain(u, carry):
        chunk_step(u, 0)
        for i in range(FAR):
            dp_tick(seqs * PER + FAR * (u - quarter - 3) + i)
        return carry

    last = max(na, nb) + 5 * LAG - seqs * PER
    steps = max(2 * nblk + 1, quarter + 3 - (-last // FAR) if grid else 0)
    lax.fori_loop(quarter + 3, steps, drain, 0)


def tail_kernel(
    blk, gtok, g, blk_out, gtok_out, gfc2, gfc1, gqkv, gdense, v0, v1, v2, v3, v4, v5, gb, sems
):
    F, D, W = gfc2.shape[0], gfc1.shape[0], gdense.shape[0]
    copies = []

    def out(src, dst):
        for k in range(2):
            rows = pl.ds(k * (dst.shape[0] // 2), dst.shape[0] // 2)
            copies.append(pltpu.make_async_copy(src.at[rows, :], dst.at[rows, :], sems.at[len(copies)]))
            copies[-1].start()

    out(blk, blk_out)
    out(gtok, gtok_out)
    out(g.at[0:F, :], gfc2)
    out(g.at[F : F + D, :], gfc1)
    out(g.at[F + D : F + D + 3 * W, :], gqkv)
    out(g.at[F + D + 3 * W : F + D + 4 * W, :], gdense)
    at_vec = F + D + 4 * W
    for i, v in enumerate((v0, v1, v2, v3, v4, v5)):
        v[...] = g[at_vec + i]
    for c in range(3):
        gb[c : c + 1, :] = g[at_vec + 6 : at_vec + 7, c * W : (c + 1) * W]
    for c in copies:
        c.wait()


def tail(blk, gtok, g, F, W):
    n, D = blk.shape
    sd = jax.ShapeDtypeStruct
    here, there = pl.BlockSpec(memory_space=VMEM), pl.BlockSpec(memory_space=pl.ANY)
    return pl.pallas_call(
        tail_kernel,
        out_shape=(
            sd((n, D), BF), sd((n, D), BF), sd((F, D), F32), sd((D, F), F32), sd((3 * W, D), F32),
            sd((W, D), F32), *([sd((D,), F32)] * 6), sd((3, W), F32),
        ),
        in_specs=[here] * 3,
        out_specs=[there] * 6 + [here] * 7,
        scratch_shapes=[pltpu.SemaphoreType.DMA((12,))],
        compiler_params=pltpu.CompilerParams(vmem_limit_bytes=2**20),
        name="tail",
    )(blk, gtok, g)


def block(grid, tokens, vectors, wqkvT, bqkv, wdense, wfc1, wfc2, cot):
    n, D = tokens.shape
    W = wdense.shape[0]
    heads = W // HD
    F = wfc1.shape[1]
    angle = np.arange(LEN, dtype=np.float64)[None, :] / 10000.0 ** (
        np.arange(0, ROT, 2, dtype=np.float64)[:, None] / ROT
    )
    cosT = jnp.asarray(np.cos(angle), F32)
    sinT = jnp.asarray(np.sin(angle), F32)
    g1, b1, g2, b2, bfc1, ob = vectors
    pairs = (F + D + 4 * W) // (2 * RC)
    na, nb = pairs + 1, pairs
    rows = (na + nb) * RC
    half, DMA = RC // 2, pltpu.SemaphoreType.DMA
    sd = jax.ShapeDtypeStruct
    inputs = (tokens, g1, b1, g2, b2, wqkvT, bqkv, wdense, wfc1, bfc1, wfc2, ob, cot, cosT, sinT)
    nch = 2 * n // CH
    return pl.pallas_call(
        lambda *refs: block_kernel(grid, *refs),
        out_shape=(VMEM((n, D), BF), VMEM((n, D), BF), VMEM((rows, D), F32)),
        in_specs=[pl.BlockSpec(memory_space=pl.ANY)] * len(inputs),
        out_specs=[pl.BlockSpec(memory_space=VMEM)] * 3,
        scratch_shapes=[
            VMEM((n, D), BF), VMEM((3 * W, D), BF), VMEM((3, W), F32), VMEM((W, D), BF),
            VMEM((D, F), BF), VMEM((F, D), BF), VMEM((n, D), BF),
            VMEM((ROT // 2, LEN), F32), VMEM((ROT // 2, LEN), F32), *([VMEM((D,), F32)] * 4),
            VMEM((F,), F32), VMEM((D,), F32), VMEM((3 * W, 1), F32),
            VMEM((QB, D), BF), VMEM((n, F), BF),
            VMEM((W, LEN), BF), VMEM((W, LEN), BF), VMEM((W, LEN), BF), VMEM((W, LEN), BF),
            VMEM((heads, LEN, HD), BF), VMEM((heads, LEN, HD), BF),
            VMEM((heads, LEN, HD), BF), VMEM((heads, LEN, HD), BF),
            VMEM((W, LEN), BF), VMEM((W, LEN), F32),
            VMEM((heads, LEN, HD), F32), VMEM((heads, LEN, HD), F32),
            VMEM((3 * W, LEN), BF), VMEM((8, 8, D), F32),
            VMEM((2 * n, D), F32),
            VMEM((SLOTS * CH // 2, D), F32), VMEM((LANDS * CH // 2, D), F32),
            VMEM((8, D), F32), VMEM((8, D), F32), VMEM((8, D), F32),
            VMEM((RING * half, D), F32), VMEM((RING * half, D), F32), VMEM((RING * half, D), F32),
            VMEM((RING * RC, D), F32), VMEM((RING * half, D), F32), VMEM((RING * half, D), F32),
            DMA((24,)), DMA((3, nch)), DMA((3, nch)), DMA((2,)), DMA((2,)),
            DMA((5, SEMS)), DMA((5, SEMS)), DMA((6, SEMS)), DMA((6, SEMS)),
            pltpu.SemaphoreType.REGULAR, pltpu.SemaphoreType.REGULAR((4,)),
        ],
        compiler_params=pltpu.CompilerParams(
            vmem_limit_bytes=SCOPED, collective_id=0, has_side_effects=True
        ),
        name="block",
    )(*inputs)


def on_device(
    grid, tokens, attention_norm_gain, attention_norm_bias, feedforward_norm_gain,
    feedforward_norm_bias, w_qkv, b_qkv, w_dense, w_fc1, b_fc1, w_fc2, out_bias, cotangent,
):
    D = tokens.shape[1]
    W, F = w_dense.shape[0], w_fc1.shape[1]
    wqkvT = jnp.transpose(w_qkv, (1, 2, 0)).reshape(3 * W, D)
    vectors = (
        attention_norm_gain, attention_norm_bias, feedforward_norm_gain, feedforward_norm_bias,
        b_fc1, out_bias,
    )
    block_out, grad_tokens, grads = block(
        grid, tokens, vectors, wqkvT, b_qkv, w_dense, w_fc1, w_fc2, cotangent
    )
    if not grid:
        grads = lax.psum(grads, "dp")
    blk, gtok, gfc2, gfc1, gqkvT, gdense, v0, v1, v2, v3, v4, v5, gb = tail(
        block_out, grad_tokens, grads, F, W
    )
    gqkv = jnp.transpose(gqkvT.reshape(3, W, D), (2, 0, 1))
    return (blk, gtok, v0, v1, v2, v3, gqkv, gb, gdense, gfc1, v4, gfc2, v5)


def solution(mesh):
    placed = (
        P("dp", None), P(), P(), P(), P(), P(None, None, "tensor"), P(None, "tensor"),
        P("tensor", None), P(None, "tensor"), P("tensor"), P("tensor", None), P(), P("dp", None),
    )
    grid = mesh.shape["dp"] == 8
    return jax.shard_map(
        lambda *args: on_device(grid, *args), mesh=mesh, in_specs=placed,
        out_specs=(
            P("dp", None), P("dp", None), P(), P(), P(), P(), P(None, None, "tensor"),
            P(None, "tensor"), P("tensor", None), P(None, "tensor"), P("tensor"),
            P("tensor", None), P(),
        ),
        check_vma=False,
    )
```

```python
import math

import jax
import jax.numpy as jnp
import numpy as np
from jax import lax
from jax.experimental import pallas as pl
from jax.experimental.pallas import tpu as pltpu
from jax.sharding import PartitionSpec as P

HD = 64
ROT = 16
LEN = 1024
QB = 256
TB = 256
CH = 256
RC = 48
LANDS = 12
SLOTS = 4
RING = 8
SEMS = 11
LAG = 2
SCOPED = 50 * 2**20
TICKS = ((None, 0), (1, 2), (3, 4), (5, 6))
PER = 8
LEAD = 4
FAR = 2
MESH = pl.DeviceIdType.MESH
BF = jnp.bfloat16
F32 = jnp.float32
ROOT_HALF = 0.7071067811865476
ROOT_TAU_INV = 0.3989422804014327
LOG2E = 1.4426950408889634
SCALE = HD ** (-0.5)
VMEM = pltpu.VMEM


def nn(a, b):
    return lax.dot_general(a, b, (((1,), (0,)), ((), ())), preferred_element_type=F32)


def nt(a, b):
    return lax.dot_general(a, b, (((1,), (1,)), ((), ())), preferred_element_type=F32)


def tn(a, b):
    return lax.dot_general(a, b, (((0,), (0,)), ((), ())), preferred_element_type=F32)


def rowsum(v):
    return jnp.sum(v.reshape(v.shape[0] // 8, 8, v.shape[1]), 0)


def standardize(rows):
    x = rows.astype(F32)
    centered = x - jnp.mean(x, -1, keepdims=True)
    inv = lax.rsqrt(jnp.mean(centered * centered, -1, keepdims=True) + 1e-5)
    return centered * inv, inv


def when(cond, f):
    pl.when(cond)(f)


class Ranks:
    def __init__(self, grid):
        t = lax.axis_index("tensor")
        d = lax.axis_index("dp")
        self.core = t % 2
        self.sib = {"tensor": t + 1 - 2 * (t % 2)}
        self.ypeer = {"tensor": (t + 2) % 4}
        self.x = d % 2
        z = d // 2
        self.xpeer = {"dp": d + 1 - 2 * (d % 2)}
        self.zpeer = {"dp": d + 2 - 4 * (z % 2)}
        self.mpeer = {"dp": (3 - z) * 2 + d % 2}
        self.center = ((z + 1) // 2) % 2
        self.hm = (z // 2) % 2
        self.grid = grid

    def greet(self):
        peers = [self.sib, self.ypeer]
        if self.grid:
            peers += [self.xpeer, self.zpeer, self.mpeer]
        sem = pltpu.get_barrier_semaphore()
        for peer in peers:
            pl.semaphore_signal(sem, inc=1, device_id=peer, device_id_type=MESH)
        return lambda: pl.semaphore_wait(sem, len(peers))


def at(start, size):
    return pl.ds(pl.multiple_of(start, 8), size)


def copy(src, dst, send, recv, peer):
    return pltpu.make_async_remote_copy(
        src_ref=src, dst_ref=dst, send_sem=send, recv_sem=recv, device_id=peer,
        device_id_type=MESH,
    )


def tell(sem, peer):
    pl.semaphore_signal(sem, inc=1, device_id=peer, device_id_type=MESH)


def add_into(dst, rows, src, srows):
    dst[rows, :] = dst[rows, :] + src[srows, :]


class TensorSum:
    HALF = CH // 2

    def __init__(self, rank, pc, rc1, rc2, send, recv, free):
        self.r, self.pc, self.rc1, self.rc2 = rank, pc, rc1, rc2
        self.s, self.v, self.free = send, recv, free
        self.n = pc.shape[0] // CH

    def mine(self, j):
        return at(j * CH + self.r.core * self.HALF, self.HALF)

    def other(self, j):
        return at(j * CH + (1 - self.r.core) * self.HALF, self.HALF)

    def slot(self, j):
        return at((j % SLOTS) * self.HALF, self.HALF)

    def land(self, j):
        return at((j % LANDS) * self.HALF, self.HALF)

    def c1(self, j):
        return copy(self.pc.at[self.other(j), :], self.rc1.at[self.slot(j), :],
                    self.s.at[2, j % SLOTS], self.v.at[2, j % SLOTS], self.r.sib)

    def c2(self, j):
        return copy(self.pc.at[self.mine(j), :], self.rc2.at[self.land(j), :],
                    self.s.at[0, j], self.v.at[0, j], self.r.ypeer)

    def c3(self, j):
        return copy(self.pc.at[self.mine(j), :], self.pc.at[self.mine(j), :],
                    self.s.at[1, j], self.v.at[1, j], self.r.sib)

    def y1(self, j):
        when(j >= SLOTS, lambda: pl.semaphore_wait(self.free, 1))
        self.c1(j).start()

    def y2(self, j):
        self.c1(j).wait_recv()
        add_into(self.pc, self.mine(j), self.rc1, self.slot(j))
        self.c2(j).start()
        self.c1(j).wait_send()
        tell(self.free, self.r.sib)

    def y3(self, j, finish):
        self.c2(j).wait()
        add_into(self.pc, self.mine(j), self.rc2, self.land(j))
        when(j >= self.n - SLOTS, lambda: pl.semaphore_wait(self.free, 1))
        self.c3(j).start()
        finish(j, self.r.core)

    def y4(self, j, finish):
        self.c3(j).wait()
        finish(j, 1 - self.r.core)


class GradSum:
    HALF = RC // 2

    def __init__(self, rank, g, ax, az, am, bz, bm, bx, a_s, a_r, b_s, b_r, free, na, nb):
        self.r, self.g = rank, g
        self.ax, self.az, self.am, self.bz, self.bm, self.bx = ax, az, am, bz, bm, bx
        self.a_s, self.a_r, self.b_s, self.b_r = a_s, a_r, b_s, b_r
        self.na, self.nb, self.free = na, nb, free

    def amine(self, k):
        return at(2 * k * RC + self.r.x * self.HALF, self.HALF)

    def aother(self, k):
        return at(2 * k * RC + (1 - self.r.x) * self.HALF, self.HALF)

    def buf(self, k):
        return at((k % RING) * self.HALF, self.HALF)

    def zbuf(self, k):
        return at((k % RING) * RC, RC)

    def ac(self, kind, k):
        g, m, b = self.g, self.amine(k), self.buf(k)
        src, dst, peer = (
            (g.at[self.aother(k), :], self.ax.at[b, :], self.r.xpeer),
            (g.at[m, :], self.az.at[b, :], self.r.zpeer),
            (g.at[m, :], self.am.at[b, :], self.r.mpeer),
            (g.at[m, :], g.at[m, :], self.r.zpeer),
            (g.at[m, :], g.at[m, :], self.r.xpeer),
        )[kind]
        return copy(src, dst, self.a_s.at[kind, k % SEMS], self.a_r.at[kind, k % SEMS], peer)

    def a1(self, k):
        self.ac(0, k).start()

    def a2(self, k):
        self.ac(0, k).wait_recv()
        add_into(self.g, self.amine(k), self.ax, self.buf(k))
        when(self.r.center == 0, lambda: self.ac(1, k).start())
        self.ac(0, k).wait_send()
        tell(self.free.at[0], self.r.xpeer)

    def a3(self, k):
        @pl.when(self.r.center == 1)
        def _():
            self.ac(1, k).wait_recv()
            add_into(self.g, self.amine(k), self.az, self.buf(k))
            self.ac(2, k).start()

        @pl.when(self.r.center == 0)
        def _():
            self.ac(1, k).wait_send()
            tell(self.free.at[1], self.r.zpeer)

    def a4(self, k):
        @pl.when(self.r.center == 1)
        def _():
            self.ac(2, k).wait()
            add_into(self.g, self.amine(k), self.am, self.buf(k))
            pl.semaphore_wait(self.free.at[1], 1)
            self.ac(3, k).start()
            pl.semaphore_wait(self.free.at[0], 1)
            self.ac(4, k).start()

    def a5(self, k):
        @pl.when(self.r.center == 0)
        def _():
            self.ac(3, k).wait_recv()
            pl.semaphore_wait(self.free.at[0], 1)
            self.ac(4, k).start()

    def a6(self, k):
        self.ac(4, k).wait()
        when(self.r.center == 1, lambda: self.ac(3, k).wait_send())

    def bfull(self, k):
        return at((2 * k + 1) * RC, RC)

    def bmine(self, k):
        return at((2 * k + 1) * RC + self.r.hm * self.HALF, self.HALF)

    def bother(self, k):
        return at((2 * k + 1) * RC + (1 - self.r.hm) * self.HALF, self.HALF)

    def bc(self, kind, k):
        g, f, m, o, b = self.g, self.bfull(k), self.bmine(k), self.bother(k), self.buf(k)
        src, dst, peer = (
            (g.at[f, :], self.bz.at[self.zbuf(k), :], self.r.zpeer),
            (g.at[o, :], self.bm.at[b, :], self.r.mpeer),
            (g.at[m, :], self.bx.at[b, :], self.r.xpeer),
            (g.at[m, :], g.at[m, :], self.r.mpeer),
            (g.at[m, :], g.at[m, :], self.r.zpeer),
            (g.at[o, :], g.at[o, :], self.r.zpeer),
        )[kind]
        return copy(src, dst, self.b_s.at[kind, k % SEMS], self.b_r.at[kind, k % SEMS], peer)

    def b1(self, k):
        when(self.r.center == 0, lambda: self.bc(0, k).start())

    def b2(self, k):
        @pl.when(self.r.center == 1)
        def _():
            self.bc(0, k).wait_recv()
            add_into(self.g, self.bfull(k), self.bz, self.zbuf(k))
            self.bc(1, k).start()

        @pl.when(self.r.center == 0)
        def _():
            self.bc(0, k).wait_send()
            tell(self.free.at[2], self.r.zpeer)

    def b3(self, k):
        @pl.when(self.r.center == 1)
        def _():
            self.bc(1, k).wait_recv()
            add_into(self.g, self.bmine(k), self.bm, self.buf(k))
            self.bc(2, k).start()
            self.bc(1, k).wait_send()
            tell(self.free.at[3], self.r.mpeer)

    def b4(self, k):
        @pl.when(self.r.center == 1)
        def _():
            self.bc(2, k).wait()
            add_into(self.g, self.bmine(k), self.bx, self.buf(k))
            pl.semaphore_wait(self.free.at[3], 1)
            self.bc(3, k).start()
            pl.semaphore_wait(self.free.at[2], 1)
            self.bc(4, k).start()

    def b5(self, k):
        @pl.when(self.r.center == 1)
        def _():
            self.bc(3, k).wait_recv()
            self.bc(5, k).start()

    def b6(self, k):
        @pl.when(self.r.center == 1)
        def _():
            self.bc(3, k).wait_send()
            self.bc(4, k).wait_send()
            self.bc(5, k).wait_send()

        @pl.when(self.r.center == 0)
        def _():
            self.bc(4, k).wait_recv()
            self.bc(5, k).wait_recv()

    def tick(self, t):
        for n, stages in ((self.na, (self.a1, self.a2, self.a3, self.a4, self.a5, self.a6)),
                          (self.nb, (self.b1, self.b2, self.b3, self.b4, self.b5, self.b6))):
            for back in range(5, -1, -1):
                k = t - LAG * back
                when(jnp.logical_and(k >= 0, k < n), lambda f=stages[back], k=k: f(k))


def block_kernel(
    grid, tokens_in, gain1_in, bias1_in, gain2_in, bias2_in, wqkvT_in, bqkv_in, wdense_in, wfc1_in,
    bfc1_in, wfc2_in, obias_in, cot_in, cosT_in, sinT_in,
    blk, gtok, g,
    tokens, wqkvT, bq, wdense, wfc1, wfc2, cot, cosT, sinT, gain1, bias1, gain2, bias2, bfc1, obias,
    bqkv, stash, gpre, qT, kT, vT, gAT, qn, kn, vn, gAn, attT, dqT, dk, dv, gT, acc,
    pc, rc1, rc2, vs, vr1, vr2, ax, az, am, bz, bm, bx,
    i_s, y_s, y_r, v_s, v_r, a_s, a_r, b_s, b_r, y_f, d_f,
):
    n, D = tokens.shape
    seqs = n // LEN
    W = wdense.shape[0]
    F = wfc1.shape[1]
    heads = W // HD
    nblk = n // CH
    pairs = (F + D + 4 * W) // (2 * RC)
    na, nb = pairs + 1, pairs
    r_fc2, r_fc1, r_qkv, r_dense, r_vec = 0, F, F + D, F + D + 3 * W, F + D + 4 * W
    hid2, act = blk, gtok
    hid1 = act

    part_rows = n // 4
    loads = [(tokens_in, tokens, 0)]
    loads += [(a, b, None) for a, b in (
        (gain2_in, gain2), (bias2_in, bias2), (wfc1_in, wfc1), (bfc1_in, bfc1), (wfc2_in, wfc2))]
    loads += [(cot_in, cot, 0)]
    loads += [(a, b, k) for k in range(1, 4) for a, b in ((tokens_in, tokens), (cot_in, cot))]
    early = len(loads)
    loads += [(a, b, None) for a, b in (
        (gain1_in, gain1), (bias1_in, bias1), (wqkvT_in, wqkvT), (bqkv_in, bq), (wdense_in, wdense),
        (cosT_in, cosT), (sinT_in, sinT), (obias_in, obias))]
    ins = []
    for i, (a, b, k) in enumerate(loads):
        if k is not None:
            a, b = a.at[pl.ds(k * part_rows, part_rows), :], b.at[pl.ds(k * part_rows, part_rows), :]
        ins.append(pltpu.make_async_copy(a, b, i_s.at[i]))
        ins[-1].start()

    rank = Ranks(grid)
    all_here = rank.greet()
    ts = TensorSum(rank, pc, rc1, rc2, y_s, y_r, y_f)
    gs = GradSum(rank, g, ax, az, am, bz, bm, bx, a_s, a_r, b_s, b_r, d_f, na, nb)

    def dp_tick(t):
        if grid:
            gs.tick(t)

    acc[...] = jnp.zeros_like(acc)
    g[at(r_qkv, g.shape[0] - r_qkv), :] = jnp.zeros((g.shape[0] - r_qkv, D), F32)

    for c in ins[:7]:
        c.wait()

    def tile(i, carry):
        rows = at(i * TB, TB)
        xhat, _ = standardize(tokens[rows, :])
        h2 = (xhat * gain2[...][None, :] + bias2[...][None, :]).astype(BF)
        hid2[rows, :] = h2
        pre = nn(h2, wfc1[...]) + bfc1[...][None, :]
        cdf = 0.5 * (1.0 + lax.erf(pre * ROOT_HALF))
        a = (pre * cdf).astype(BF)
        act[rows, :] = a
        slope = cdf + pre * jnp.exp(-0.5 * pre * pre) * ROOT_TAU_INV
        ct = cot[rows, :]
        gp = (nt(ct, wfc2[...]) * slope).astype(BF)
        gpre[rows, :] = gp
        out = at(i * TB + (i // (LEN // TB)) * LEN, TB)
        pc[out, :] = nn(a, wfc2[...])
        g2 = nt(gp, wfc1[...])
        pc[at((i // (LEN // TB) + 1) * LEN + i * TB, TB), :] = g2 * gain2[...][None, :]
        acc[2] += rowsum(g2 * xhat)
        acc[3] += rowsum(g2)
        acc[4] += rowsum(gp.astype(F32))
        acc[5] += rowsum(ct.astype(F32))
        return carry

    quarter = part_rows // TB
    lax.fori_loop(0, quarter, tile, 0)
    for c in ins[7:]:
        c.wait()
    lax.fori_loop(quarter, n // TB, tile, 0)
    for part in range(3):
        row = jnp.broadcast_to(bq[part : part + 1, :], (8, W))
        bqkv[part * W : (part + 1) * W, :] = row.T[:, 0:1]

    def wgrad(lhs, rhs, row, first=0, last=None):
        def body(j, carry):
            g[at(row + j * 256, 256), :] = tn(lhs[:, pl.ds(pl.multiple_of(j * 256, 256), 256)], rhs[...])
            return carry

        lax.fori_loop(first, last or lhs.shape[1] // 256, body, 0)

    all_here()

    quarter = LEN // CH

    def finish_block(j, half):
        rows = at((j // (2 * quarter)) * LEN + (j % quarter) * CH + half * (CH // 2), CH // 2)
        summed = pc[at(j * CH + half * (CH // 2), CH // 2), :]
        blk[rows, :] = (tokens[rows, :].astype(F32) + summed + obias[...][None, :]).astype(BF)

    def finish_tokens(j, half):
        rows = at((j // (2 * quarter)) * LEN + (j % quarter) * CH + half * (CH // 2), CH // 2)
        c = pc[at(j * CH + half * (CH // 2), CH // 2), :]
        xhat, inv = standardize(tokens[rows, :])
        inside = c - jnp.mean(c, -1, keepdims=True) - xhat * jnp.mean(c * xhat, -1, keepdims=True)
        gtok[rows, :] = (cot[rows, :].astype(F32) + inv * inside).astype(BF)

    def finish(j, half):
        is_block = (j // quarter) % 2 == 0
        when(is_block, lambda: finish_block(j, half))
        when(jnp.logical_not(is_block), lambda: finish_tokens(j, half))

    def sentence(s, carry):
        base = s * LEN

        def proj(j, carry):
            cols = pl.ds(pl.multiple_of(j * QB, QB), QB)
            rows = at(base + j * QB, QB)
            c, sn = cosT[:, cols], sinT[:, cols]
            xhat, _ = standardize(tokens[rows, :])
            h1 = (xhat * gain1[...][None, :] + bias1[...][None, :]).astype(BF)
            if j == 0:
                stash[...] = h1
            else:
                hid1[rows, :] = h1
            pr = nt(wqkvT[...], h1) + bqkv[...]
            ga = nt(wdense[...], cot[rows, :]).astype(BF)
            gAT[:, cols] = ga
            for h in range(heads):
                for part, dT, dn in ((0, qT, qn), (1, kT, kn)):
                    o = part * W + h * HD
                    u, w = pr[o : o + 8], pr[o + 8 : o + 16]
                    full = jnp.concatenate(
                        [u * c - w * sn, w * c + u * sn, pr[o + 16 : o + HD]], 0
                    ).astype(BF)
                    dT[h * HD : (h + 1) * HD, cols] = full
                    dn[h, cols, :] = full.T
                o = 2 * W + h * HD
                vv = pr[o : o + HD].astype(BF)
                vT[h * HD : (h + 1) * HD, cols] = vv
                vn[h, cols, :] = vv.T
                gAn[h, cols, :] = ga[h * HD : (h + 1) * HD].T
            return carry

        dk[...] = jnp.zeros_like(dk)
        dv[...] = jnp.zeros_like(dv)
        for qb in range(LEN // QB):
            proj(qb, 0)
            nk = (qb + 1) * QB
            cols = slice(qb * QB, nk)

            mid, end = TICKS[qb]

            def head(h, carry):
                hr = pl.ds(pl.multiple_of(h * HD, HD), HD)
                st = nn(kn[h, :nk, :], qT[hr, cols])
                key = lax.broadcasted_iota(jnp.int32, (QB, QB), 0)
                qry = lax.broadcasted_iota(jnp.int32, (QB, QB), 1)
                diag = jnp.where(key <= qry, st[nk - QB :], -1e30)
                st = jnp.concatenate([st[: nk - QB], diag], 0) if nk > QB else diag
                top = jnp.max(st, 0, keepdims=True)
                e = jnp.exp2((st - top) * (SCALE * LOG2E))
                p = e * (1.0 / jnp.sum(e, 0, keepdims=True))
                low = p.astype(BF)
                attT[hr, cols] = nn(vT[hr, :nk], low).astype(BF)
                gp = nn(vn[h, :nk, :], gAT[hr, cols])
                inner = jnp.sum(p * gp, 0, keepdims=True)
                ds = (p * (gp - inner)).astype(BF)
                dqT[hr, cols] = nn(kT[hr, :nk], ds) * SCALE
                dk[h, :nk, :] += nn(ds, qn[h, cols, :])
                dv[h, :nk, :] += nn(low, gAn[h, cols, :])
                if mid is not None:
                    when(h == 1, lambda: dp_tick(s * PER + mid))
                return carry

            lax.fori_loop(0, heads, head, 0)
            pc[at(2 * base + qb * QB, QB), :] += tn(attT[:, cols], wdense[...])
            j = s * (LEN // QB) + qb
            ts.y1(j)
            if qb == 0:
                when(s == 0, lambda: wgrad(act, cot, r_fc2, 0, 2))
                dp_tick(s * PER + end)
                ts.y2(j)
                when(s == 0, lambda: wgrad(act, cot, r_fc2, 2))
                hid1[at(base, QB), :] = stash[...]
            else:
                dp_tick(s * PER + end)
                ts.y2(j)
            if qb == 1:
                when(s == 0, lambda: wgrad(hid2, gpre, r_fc1))

            @pl.when(s > 0)
            def _():
                if qb > 0:
                    ts.y4(qb - 1, finish)
                ts.y3(qb, finish)

        def back(j, carry):
            cols = pl.ds(pl.multiple_of(j * QB, QB), QB)
            rows = at(base + j * QB, QB)
            c, sn = cosT[:, cols], sinT[:, cols]
            for h in range(heads):
                hs = slice(h * HD, (h + 1) * HD)
                for k, gr in ((0, dqT[hs, cols]), (1, dk[h, cols, :].T * SCALE)):
                    u, w = gr[0:8], gr[8:16]
                    gT[k * W + h * HD : k * W + (h + 1) * HD, cols] = jnp.concatenate(
                        [u * c + w * sn, w * c - u * sn, gr[16:]], 0
                    ).astype(BF)
                gT[2 * W + h * HD : 2 * W + (h + 1) * HD, cols] = dv[h, cols, :].T.astype(BF)
            g1 = tn(gT[:, cols], wqkvT[...])
            xhat, _ = standardize(tokens[rows, :])
            pc[at(2 * base + LEN + j * QB, QB), :] += g1 * gain1[...][None, :]
            acc[0] += rowsum(g1 * xhat)
            acc[1] += rowsum(g1)
            return carry

        lax.fori_loop(0, LEN // QB, back, 0)
        srows = at(base, LEN)
        g[at(r_qkv, 3 * W), :] += nn(gT[...], hid1[srows, :])
        g[at(r_dense, W), :] += nn(attT[...], cot[srows, :])
        ones = jnp.ones((8, LEN), BF)
        g[r_vec + 6 : r_vec + 7, 0 : 3 * W] += nt(ones, gT[...])[0:1]
        dp_tick(s * PER + PER - 1)
        return carry

    lax.fori_loop(0, seqs, sentence, 0)

    def chunk_step(u, carry, between=lambda: None):
        when(jnp.logical_and(u >= 1, u <= 2 * nblk), lambda: ts.y4(u - 1, finish))
        when(jnp.logical_and(u + LEAD >= nblk, u + LEAD < 2 * nblk), lambda: ts.y1(u + LEAD))
        between()
        when(u < 2 * nblk, lambda: ts.y3(u, finish))
        when(jnp.logical_and(u + LEAD - 1 >= nblk, u + LEAD - 1 < 2 * nblk), lambda: ts.y2(u + LEAD - 1))
        return carry

    vs[...] = jnp.sum(acc[...], 1)
    g[r_vec + 4 : r_vec + 6, :] = vs[4:6, :]
    v1 = copy(vs, vr1, v_s.at[0], v_r.at[0], rank.sib)
    v1.start()
    lax.fori_loop(quarter, quarter + 2, chunk_step, 0)
    v1.wait()
    vs[...] = vs[...] + vr1[...]
    v2 = copy(vs, vr2, v_s.at[1], v_r.at[1], rank.ypeer)
    v2.start()
    lax.fori_loop(quarter + 2, quarter + 3, chunk_step, 0)
    v2.wait()
    g[r_vec : r_vec + 4, :] = vs[0:4, :] + vr2[0:4, :]

    def drain(u, carry):
        t = seqs * PER + FAR * (u - quarter - 3)
        chunk_step(u, 0, lambda: dp_tick(t))
        dp_tick(t + 1)
        return carry

    last = max(na, nb) + 5 * LAG - seqs * PER
    steps = max(2 * nblk + 1, quarter + 3 - (-last // FAR) if grid else 0)
    lax.fori_loop(quarter + 3, steps, drain, 0)


def tail_kernel(
    blk, gtok, g, blk_out, gtok_out, gfc2, gfc1, gqkv, gdense, v0, v1, v2, v3, v4, v5, gb, sems
):
    F, D, W = gfc2.shape[0], gfc1.shape[0], gdense.shape[0]
    copies = []

    def out(src, dst):
        for k in range(4):
            rows = pl.ds(k * (dst.shape[0] // 4), dst.shape[0] // 4)
            copies.append(pltpu.make_async_copy(src.at[rows, :], dst.at[rows, :], sems.at[len(copies)]))
            copies[-1].start()

    out(blk, blk_out)
    out(gtok, gtok_out)
    out(g.at[0:F, :], gfc2)
    out(g.at[F : F + D, :], gfc1)
    out(g.at[F + D : F + D + 3 * W, :], gqkv)
    out(g.at[F + D + 3 * W : F + D + 4 * W, :], gdense)
    at_vec = F + D + 4 * W
    for i, v in enumerate((v0, v1, v2, v3, v4, v5)):
        v[...] = g[at_vec + i]
    for c in range(3):
        gb[c : c + 1, :] = g[at_vec + 6 : at_vec + 7, c * W : (c + 1) * W]
    for c in copies:
        c.wait()


def tail(blk, gtok, g, F, W):
    n, D = blk.shape
    sd = jax.ShapeDtypeStruct
    here, there = pl.BlockSpec(memory_space=VMEM), pl.BlockSpec(memory_space=pl.ANY)
    return pl.pallas_call(
        tail_kernel,
        out_shape=(
            sd((n, D), BF), sd((n, D), BF), sd((F, D), F32), sd((D, F), F32), sd((3 * W, D), F32),
            sd((W, D), F32), *([sd((D,), F32)] * 6), sd((3, W), F32),
        ),
        in_specs=[here] * 3,
        out_specs=[there] * 6 + [here] * 7,
        scratch_shapes=[pltpu.SemaphoreType.DMA((24,))],
        compiler_params=pltpu.CompilerParams(vmem_limit_bytes=2**20),
        name="tail",
    )(blk, gtok, g)


def block(grid, tokens, vectors, wqkvT, bqkv, wdense, wfc1, wfc2, cot):
    n, D = tokens.shape
    W = wdense.shape[0]
    heads = W // HD
    F = wfc1.shape[1]
    angle = np.arange(LEN, dtype=np.float64)[None, :] / 10000.0 ** (
        np.arange(0, ROT, 2, dtype=np.float64)[:, None] / ROT
    )
    cosT = jnp.asarray(np.cos(angle), F32)
    sinT = jnp.asarray(np.sin(angle), F32)
    g1, b1, g2, b2, bfc1, ob = vectors
    pairs = (F + D + 4 * W) // (2 * RC)
    na, nb = pairs + 1, pairs
    rows = (na + nb) * RC
    half, DMA = RC // 2, pltpu.SemaphoreType.DMA
    sd = jax.ShapeDtypeStruct
    inputs = (tokens, g1, b1, g2, b2, wqkvT, bqkv, wdense, wfc1, bfc1, wfc2, ob, cot, cosT, sinT)
    nch = 2 * n // CH
    return pl.pallas_call(
        lambda *refs: block_kernel(grid, *refs),
        out_shape=(VMEM((n, D), BF), VMEM((n, D), BF), VMEM((rows, D), F32)),
        in_specs=[pl.BlockSpec(memory_space=pl.ANY)] * len(inputs),
        out_specs=[pl.BlockSpec(memory_space=VMEM)] * 3,
        scratch_shapes=[
            VMEM((n, D), BF), VMEM((3 * W, D), BF), VMEM((3, W), F32), VMEM((W, D), BF),
            VMEM((D, F), BF), VMEM((F, D), BF), VMEM((n, D), BF),
            VMEM((ROT // 2, LEN), F32), VMEM((ROT // 2, LEN), F32), *([VMEM((D,), F32)] * 4),
            VMEM((F,), F32), VMEM((D,), F32), VMEM((3 * W, 1), F32),
            VMEM((QB, D), BF), VMEM((n, F), BF),
            VMEM((W, LEN), BF), VMEM((W, LEN), BF), VMEM((W, LEN), BF), VMEM((W, LEN), BF),
            VMEM((heads, LEN, HD), BF), VMEM((heads, LEN, HD), BF),
            VMEM((heads, LEN, HD), BF), VMEM((heads, LEN, HD), BF),
            VMEM((W, LEN), BF), VMEM((W, LEN), F32),
            VMEM((heads, LEN, HD), F32), VMEM((heads, LEN, HD), F32),
            VMEM((3 * W, LEN), BF), VMEM((8, 8, D), F32),
            VMEM((2 * n, D), F32),
            VMEM((SLOTS * CH // 2, D), F32), VMEM((LANDS * CH // 2, D), F32),
            VMEM((8, D), F32), VMEM((8, D), F32), VMEM((8, D), F32),
            VMEM((RING * half, D), F32), VMEM((RING * half, D), F32), VMEM((RING * half, D), F32),
            VMEM((RING * RC, D), F32), VMEM((RING * half, D), F32), VMEM((RING * half, D), F32),
            DMA((24,)), DMA((3, nch)), DMA((3, nch)), DMA((2,)), DMA((2,)),
            DMA((5, SEMS)), DMA((5, SEMS)), DMA((6, SEMS)), DMA((6, SEMS)),
            pltpu.SemaphoreType.REGULAR, pltpu.SemaphoreType.REGULAR((4,)),
        ],
        compiler_params=pltpu.CompilerParams(
            vmem_limit_bytes=SCOPED, collective_id=0, has_side_effects=True
        ),
        name="block",
    )(*inputs)


def on_device(
    grid, tokens, attention_norm_gain, attention_norm_bias, feedforward_norm_gain,
    feedforward_norm_bias, w_qkv, b_qkv, w_dense, w_fc1, b_fc1, w_fc2, out_bias, cotangent,
):
    D = tokens.shape[1]
    W, F = w_dense.shape[0], w_fc1.shape[1]
    wqkvT = jnp.transpose(w_qkv, (1, 2, 0)).reshape(3 * W, D)
    vectors = (
        attention_norm_gain, attention_norm_bias, feedforward_norm_gain, feedforward_norm_bias,
        b_fc1, out_bias,
    )
    block_out, grad_tokens, grads = block(
        grid, tokens, vectors, wqkvT, b_qkv, w_dense, w_fc1, w_fc2, cotangent
    )
    if not grid:
        grads = lax.psum(grads, "dp")
    blk, gtok, gfc2, gfc1, gqkvT, gdense, v0, v1, v2, v3, v4, v5, gb = tail(
        block_out, grad_tokens, grads, F, W
    )
    gqkv = jnp.transpose(gqkvT.reshape(3, W, D), (2, 0, 1))
    return (blk, gtok, v0, v1, v2, v3, gqkv, gb, gdense, gfc1, v4, gfc2, v5)


def solution(mesh):
    placed = (
        P("dp", None), P(), P(), P(), P(), P(None, None, "tensor"), P(None, "tensor"),
        P("tensor", None), P(None, "tensor"), P("tensor"), P("tensor", None), P(), P("dp", None),
    )
    grid = mesh.shape["dp"] == 8
    return jax.shard_map(
        lambda *args: on_device(grid, *args), mesh=mesh, in_specs=placed,
        out_specs=(
            P("dp", None), P("dp", None), P(), P(), P(), P(), P(None, None, "tensor"),
            P(None, "tensor"), P("tensor", None), P(None, "tensor"), P("tensor"),
            P("tensor", None), P(),
        ),
        check_vma=False,
    )
```
